512 devices in a mesh: src: 32 (over y, x, core), tgt: 16 (over z).
Axes of the slice: x: 4, y: 4, z: 16, core: 2. Of those that a mesh axis runs over, the one named last changes fastest.
Arguments:
- src_cells: float32 [50, 131072], P(None, ('src', 'tgt')), may hold values from -0.8 to 0.8
- tgt_cells: float32 [50, 8192], P(None, 'tgt'), may hold values from -0.8 to 0.8
- src_mass: float32 [131072], P('src'), may hold values from 0.5 to 2
- tgt_mass: float32 [8192], P('tgt'), may hold values from 0.5 to 2
Outputs:
- src_potential: float32 [131072], P('src')
- tgt_potential: float32 [8192], P('tgt')
The draws below stay inside these ranges and needn't reach their ends.
All inputs are finite; a program needn't handle non-finite values.
Results may differ from the reference program's by a relative error of at most 0.00015.
Values sent between devices are 32-bit elements; how exact they have to be, the bound alone decides.
No kernel may reach another device: no remote copies, remote signals or barrier semaphores. Data moves between devices by JAX's collectives and lax.ppermute only.
A program may use at most 64 MiB of HBM per device.

```python
import math
import jax
import jax.numpy as jnp
from jax import lax

PC = 50
SRC_DEV = 4096
ITERS = 2
NS = 131072
NT = 8192


def cell_draw(base_key, salt, column_count):
    draw_key = jax.random.fold_in(base_key, salt)
    return jax.random.uniform(draw_key, (PC, column_count), jnp.float32, -0.8, 0.8)


def draw_src_cells(key, part):
    return cell_draw(key, 11, NS)


def draw_tgt_cells(key, part):
    return cell_draw(key, 23, NT)


def block_scale(rng, shape, pieces, smallest, largest):
    level, own = 1.0, jax.random.fold_in(rng, 6)
    for dim, shards_of in pieces:
        heights = jnp.exp(jax.random.uniform(jax.random.fold_in(own, dim), (shards_of,), jnp.float32, smallest / len(pieces), largest / len(pieces)))
        level = level * jnp.repeat(heights, shape[dim] // shards_of).reshape([-1 if axis == dim else 1 for axis in range(len(shape))])
    return level


def setup_inputs(seed: int = 0) -> dict:
    splits = jax.random.split(jax.random.key(seed), 5)
    src_cells = draw_src_cells(jax.random.fold_in(splits[4], 71), 0)
    tgt_cells = draw_tgt_cells(jax.random.fold_in(splits[4], 71), 0)
    src_mass = jnp.clip(jnp.exp(math.log(2.0) - 1.3862944 * jax.random.uniform(splits[2], (NS,), jnp.float32) ** block_scale(splits[2], (NS,), ((0, 32),), -0.2, 0.2)), 0.5, 2.0)
    tgt_mass = jnp.clip(jnp.exp(math.log(2.0) - 1.3862944 * jax.random.uniform(splits[3], (NT,), jnp.float32) ** block_scale(splits[3], (NT,), ((0, 16),), -0.2, 0.2)), 0.5, 2.0)
    return dict(src_cells=src_cells, tgt_cells=tgt_cells, src_mass=src_mass, tgt_mass=tgt_mass)


epsilon_reg = 2.0


def gibbs_tile(src_block, tgt_block):
    src_norm = jnp.sum(src_block * src_block, axis=0)
    tgt_norm = jnp.sum(tgt_block * tgt_block, axis=0)
    cross = jnp.dot(src_block.T, tgt_block, precision=lax.Precision.HIGHEST, preferred_element_type=jnp.float32)
    cost = src_norm[:, None] + tgt_norm[None, :] - 2.0 * cross
    return jnp.exp(-cost / epsilon_reg)


def reference(src_cells, tgt_cells, src_mass, tgt_mass):
    blocks = NS // SRC_DEV
    src_blocks = jnp.transpose(src_cells.reshape(PC, blocks, SRC_DEV), (1, 0, 2))
    col_scale = jnp.ones((NT,), jnp.float32)
    row_scale = jnp.ones((NS,), jnp.float32)
    for sweep in range(ITERS):
        def row_pass(src_block):
            return jnp.dot(gibbs_tile(src_block, tgt_cells), col_scale, precision=lax.Precision.HIGHEST)
        row_total = lax.map(row_pass, src_blocks).reshape(NS)
        row_scale = src_mass / row_total
        row_parts = row_scale.reshape(blocks, SRC_DEV)

        def col_pass(total, pair):
            src_block, weights = pair
            return total + jnp.dot(weights, gibbs_tile(src_block, tgt_cells), precision=lax.Precision.HIGHEST), None
        col_total, unused = lax.scan(col_pass, jnp.zeros((NT,), jnp.float32), (src_blocks, row_parts))
        col_scale = tgt_mass / col_total
    return epsilon_reg * jnp.log(row_scale), epsilon_reg * jnp.log(col_scale)
```

```python
import jax
import jax.numpy as jnp
from jax import lax
from jax.experimental import pallas as pl
from jax.experimental.pallas import tpu as pltpu
from jax.sharding import Mesh, PartitionSpec as P

NY, NX, NC, NZ = 4, 4, 2, 16
NG = NX * NC
PLANE = ("y", "x", "core")
GROUP = ("x", "core")
PC = 50
HALF = 26
MASS = 56
ROWS, COLS = 2048, 1024
PIECE = 64
OWN = 256
EPS = 2.0


def split(value):
    high = value.astype(jnp.bfloat16)
    low = (value - high.astype(jnp.float32)).astype(jnp.bfloat16)
    return high, low


def pieces(norm):
    first = norm.astype(jnp.bfloat16).astype(jnp.float32)
    rest = norm - first
    second = rest.astype(jnp.bfloat16).astype(jnp.float32)
    return first, second, rest - second


def masked(cells):
    row = lax.broadcasted_iota(jnp.int32, cells.shape, 0)
    keep = (row < HALF) | ((row >= 32) & (row < 32 + PC - HALF))
    return row, jnp.where(keep, cells, 0.0)


def gibbs_kernel(rows_ref, cols_ref, gibbs_ref, part_ref, row_mass_ref, col_mass_ref, x_ref, y_ref):
    for g in range(NG):
        here = slice(g * OWN, (g + 1) * OWN)
        cells = rows_ref[g]
        row_mass_ref[:, here] = cells[MASS : MASS + 1]
        row, cells = masked(cells)
        first, second, third = pieces(-0.5 * jnp.sum(cells * cells, axis=0, keepdims=True))
        high, low = split(cells)
        extra = jnp.where(row == 26, first, jnp.where(row == 27, second, jnp.where(row == 28, third, 0.0)))
        extra = jnp.where((row >= 29) & (row < 32), 1.0, extra)
        x_ref[0:64, here] = (high.astype(jnp.float32) + extra).astype(jnp.bfloat16)
        x_ref[64:128, here] = high
        x_ref[128:192, here] = low
        x_ref[192:256, here] = low
    lane = lax.broadcasted_iota(jnp.int32, (32, 128), 1)
    for t in range(NZ // 2):
        here = slice(t * 128, (t + 1) * 128)
        a, b = cols_ref[2 * t], cols_ref[2 * t + 1]
        top = jnp.where(lane < 64, a, pltpu.roll(b, 64, 1))
        bottom = jnp.where(lane < 64, pltpu.roll(a, 64, 1), b)
        col_mass_ref[:, here] = bottom[MASS - 32 : MASS - 31]
        row, cells = masked(jnp.concatenate([top, bottom], axis=0))
        first, second, third = pieces(-0.5 * jnp.sum(cells * cells, axis=0, keepdims=True))
        high, low = split(cells)
        extra = jnp.where(row == 29, first, jnp.where(row == 30, second, jnp.where(row == 31, third, 0.0)))
        extra = jnp.where((row >= 26) & (row < 29), 1.0, extra)
        both = jnp.concatenate([high.astype(jnp.float32) + extra, low.astype(jnp.float32)], axis=0)
        turned = both.T.astype(jnp.bfloat16)
        y_ref[here, 0:128] = turned
        y_ref[here, 128:256] = turned
    for n in range(ROWS // 256):
        there = slice(n * 256, (n + 1) * 256)
        total = jnp.zeros((8, 256), jnp.float32)
        for m in range(COLS // 256):
            here = slice(m * 256, (m + 1) * 256)
            tile = jnp.exp(jnp.dot(y_ref[here, :], x_ref[:, there], preferred_element_type=jnp.float32))
            gibbs_ref[here, there] = tile
            total = total + jnp.sum(tile.reshape(32, 8, 256), axis=0)
        part_ref[:, there] = jnp.sum(total, axis=0, keepdims=True)


def column_kernel(gibbs_ref, parts_ref, mass_ref, part_ref, scale_ref):
    scale_ref[...] = mass_ref[...] / jnp.sum(parts_ref[...], axis=0, keepdims=True)
    for j in range(COLS // 128):
        here = slice(j * 128, (j + 1) * 128)
        total = jnp.zeros((128, 128), jnp.float32)
        for i in range(ROWS // 128):
            there = slice(i * 128, (i + 1) * 128)
            total = total + gibbs_ref[here, there] * scale_ref[:, there]
        part_ref[:, here] = jnp.sum(total.T, axis=0, keepdims=True)


def row_kernel(gibbs_ref, parts_ref, mass_ref, part_ref):
    scale = mass_ref[...] / jnp.sum(parts_ref[...], axis=0, keepdims=True)
    totals = [jnp.zeros((8, 128), jnp.float32)] * (ROWS // 128)
    for j in range(COLS // 128):
        here = slice(j * 128, (j + 1) * 128)
        spread = jnp.broadcast_to(scale[:, here], (128, 128)).T
        for i in range(ROWS // 128):
            there = slice(i * 128, (i + 1) * 128)
            totals[i] = totals[i] + jnp.sum((gibbs_ref[here, there] * spread).reshape(16, 8, 128), axis=0)
    for i in range(ROWS // 128):
        part_ref[:, i * 128 : (i + 1) * 128] = jnp.sum(totals[i], axis=0, keepdims=True)


def f32(*shape):
    return jax.ShapeDtypeStruct(shape, jnp.float32)


def call(kernel, outs, *args, scratch=()):
    whole = pl.BlockSpec(memory_space=pltpu.VMEM)
    return pl.pallas_call(
        kernel,
        out_shape=outs,
        in_specs=[whole] * len(args),
        out_specs=[whole] * len(outs),
        scratch_shapes=list(scratch),
        compiler_params=pltpu.CompilerParams(vmem_limit_bytes=24 << 20),
    )(*args)


def swap(value, axes):
    return lax.all_to_all(value, axes, 0, 0, tiled=True)


def gather(value, axes, count):
    return swap(jnp.broadcast_to(value[None], (count,) + value.shape), axes)


def local(src_cells, tgt_cells, src_mass, tgt_mass):
    me = lax.axis_index("x") * NC + lax.axis_index("core")
    own_mass = lax.dynamic_slice(src_mass, (lax.axis_index("z") * OWN,), (OWN,))
    gap = jnp.zeros((6, OWN), jnp.float32)
    rows = jnp.concatenate(
        [src_cells[:HALF], gap, src_cells[HALF:], own_mass[None], gap, gap[:1]], axis=0
    )
    piece = lax.dynamic_slice(tgt_cells, (0, me * PIECE), (PC, PIECE))
    piece_mass = lax.dynamic_slice(tgt_mass, (me * PIECE,), (PIECE,))
    bottom = jnp.concatenate([piece[HALF:], piece_mass[None], jnp.zeros((1, PIECE), jnp.float32)], axis=0)
    cols = jnp.concatenate([piece[:HALF], bottom], axis=1)
    cols = gather(cols.reshape(HALF * 128), "z", NZ).reshape(NZ, HALF, 128)
    cols = jnp.pad(cols, ((0, 0), (0, 32 - HALF), (0, 0)))
    rows = gather(rows, GROUP, NG)

    gibbs, row_part, row_mass, col_mass = call(
        gibbs_kernel,
        (f32(COLS, ROWS), f32(1, ROWS), f32(1, ROWS), f32(1, COLS)),
        rows,
        cols,
        scratch=(pltpu.VMEM((256, ROWS), jnp.bfloat16), pltpu.VMEM((COLS, 256), jnp.bfloat16)),
    )
    outs = (f32(1, COLS), f32(1, ROWS))
    row_parts = gather(row_part[0], GROUP, NG)
    col_part, _ = call(column_kernel, outs, gibbs, row_parts, row_mass)
    col_part = jnp.sum(gather(col_part[0], "y", NY), axis=0)
    col_parts = gather(col_part, "z", NZ)
    (row_part,) = call(row_kernel, (f32(1, ROWS),), gibbs, col_parts, col_mass)
    row_parts = gather(row_part[0], GROUP, NG)
    col_part, row_scale = call(column_kernel, outs, gibbs, row_parts, row_mass)

    own_scale = lax.dynamic_slice(row_scale[0], (me * OWN,), (OWN,))
    leaving = jnp.concatenate(
        [col_part.reshape(NZ, PIECE), jnp.broadcast_to(own_scale[None], (NZ, OWN))], axis=1
    )
    landed = swap(leaving, "z")
    row_out = EPS * jnp.log(landed[:, PIECE:].reshape(NZ * OWN))
    col_part = gather(jnp.sum(landed[:, :PIECE], axis=0), PLANE, NY * NG)
    col_total = jnp.sum(col_part.reshape(NY, NG * PIECE), axis=0)
    return row_out, EPS * jnp.log(tgt_mass / col_total)


def solution(mesh):
    grid = Mesh(mesh.devices.reshape(NY, NX, NC, NZ), ("y", "x", "core", "z"))
    placed = (P(None, PLANE + ("z",)), P(None, "z"), P(PLANE), P("z"))
    return jax.shard_map(local, mesh=grid, in_specs=placed, out_specs=(P(PLANE), P("z")), check_vma=False)
```

```python
import jax
import jax.numpy as jnp
from jax import lax
from jax.experimental import pallas as pl
from jax.experimental.pallas import tpu as pltpu
from jax.sharding import Mesh, PartitionSpec as P

NY, NX, NC, NZ = 4, 4, 2, 16
NG = NX * NC
PLANE = ("y", "x", "core")
GROUP = ("x", "core")
PC = 50
HALF = 26
MASS = 56
ROWS, COLS = 2048, 1024
PIECE = 64
OWN = 256
EPS = 2.0


def split(value):
    high = value.astype(jnp.bfloat16)
    low = (value - high.astype(jnp.float32)).astype(jnp.bfloat16)
    return high, low


def pieces(norm):
    first = norm.astype(jnp.bfloat16).astype(jnp.float32)
    rest = norm - first
    second = rest.astype(jnp.bfloat16).astype(jnp.float32)
    return first, second, rest - second


def masked(cells):
    row = lax.broadcasted_iota(jnp.int32, cells.shape, 0)
    keep = (row < HALF) | ((row >= 32) & (row < 32 + PC - HALF))
    return row, jnp.where(keep, cells, 0.0)


def pack_kernel(src_ref, tgt_ref, src_mass_ref, tgt_mass_ref, rows_ref, cols_ref):
    x, core, z = (lax.axis_index(name) for name in ("x", "core", "z"))
    rows_ref[...] = jnp.zeros_like(rows_ref)
    rows_ref[0:HALF] = src_ref[0:HALF]
    rows_ref[32 : 32 + PC - HALF] = src_ref[HALF:PC]
    for k in range(2):
        rows_ref[MASS : MASS + 1, k * 128 : (k + 1) * 128] = src_mass_ref[pl.ds(2 * z + k, 1)]
    here = pl.ds(pl.multiple_of(x * 128, 128), 128)
    cells = tgt_ref[:, here]
    top = cells[0:HALF]
    bottom = jnp.concatenate([cells[HALF:PC], tgt_mass_ref[pl.ds(x, 1)], jnp.zeros((1, 128), jnp.float32)], axis=0)
    lane = lax.broadcasted_iota(jnp.int32, (HALF, 128), 1)
    first = jnp.where(lane < PIECE, top, pltpu.roll(bottom, PIECE, 1))
    second = jnp.where(lane < PIECE, pltpu.roll(top, PIECE, 1), bottom)
    piece = jnp.where(jnp.broadcast_to(core, (HALF, 128)) == 0, first, second)
    for k in range(NZ):
        cols_ref[k * HALF : (k + 1) * HALF] = piece


def gibbs_kernel(own_ref, one_ref, two_ref, three_ref, cols_ref, gibbs_ref, part_ref, row_mass_ref, col_mass_ref, x_ref, y_ref):
    x = lax.axis_index("x")
    for k, rows_ref in enumerate((own_ref, one_ref, two_ref, three_ref)):
        base = pl.multiple_of(lax.rem(x + NX - k, NX) * (NC * OWN), NC * OWN)
        for c in range(NC):
            here = pl.ds(pl.multiple_of(base + c * OWN, OWN), OWN)
            cells = rows_ref[c]
            row_mass_ref[:, here] = cells[MASS : MASS + 1]
            row, cells = masked(cells)
            first, second, third = pieces(-0.5 * jnp.sum(cells * cells, axis=0, keepdims=True))
            high, low = split(cells)
            extra = jnp.where(row == 26, first, jnp.where(row == 27, second, jnp.where(row == 28, third, 0.0)))
            extra = jnp.where((row >= 29) & (row < 32), 1.0, extra)
            x_ref[0:64, here] = (high.astype(jnp.float32) + extra).astype(jnp.bfloat16)
            x_ref[64:128, here] = high
            x_ref[128:192, here] = low
            x_ref[192:256, here] = low
    lane = lax.broadcasted_iota(jnp.int32, (32, 128), 1)
    gap = jnp.zeros((32 - HALF, 128), jnp.float32)
    for t in range(NZ // 2):
        here = slice(t * 128, (t + 1) * 128)
        a, b = (
            jnp.concatenate([cols_ref[k * HALF : (k + 1) * HALF], gap], axis=0) for k in (2 * t, 2 * t + 1)
        )
        top = jnp.where(lane < PIECE, a, pltpu.roll(b, PIECE, 1))
        bottom = jnp.where(lane < PIECE, pltpu.roll(a, PIECE, 1), b)
        col_mass_ref[:, here] = bottom[MASS - 32 : MASS - 31]
        row, cells = masked(jnp.concatenate([top, bottom], axis=0))
        first, second, third = pieces(-0.5 * jnp.sum(cells * cells, axis=0, keepdims=True))
        high, low = split(cells)
        extra = jnp.where(row == 29, first, jnp.where(row == 30, second, jnp.where(row == 31, third, 0.0)))
        extra = jnp.where((row >= 26) & (row < 29), 1.0, extra)
        both = jnp.concatenate([high.astype(jnp.float32) + extra, low.astype(jnp.float32)], axis=0)
        turned = both.T.astype(jnp.bfloat16)
        y_ref[here, 0:128] = turned
        y_ref[here, 128:256] = turned
    for n in range(ROWS // 256):
        there = slice(n * 256, (n + 1) * 256)
        total = jnp.zeros((8, 256), jnp.float32)
        for m in range(COLS // 256):
            here = slice(m * 256, (m + 1) * 256)
            tile = jnp.exp(jnp.dot(y_ref[here, :], x_ref[:, there], preferred_element_type=jnp.float32))
            gibbs_ref[here, there] = tile
            total = total + jnp.sum(tile.reshape(32, 8, 256), axis=0)
        total = jnp.sum(total, axis=0, keepdims=True)
        for k in range(NG):
            part_ref[k, :, there] = total


def summed(parts_ref):
    total = parts_ref[0]
    for k in range(1, parts_ref.shape[0]):
        total = total + parts_ref[k]
    return total


def columns(gibbs_ref, scale_ref, j):
    here = slice(j * 128, (j + 1) * 128)
    total = jnp.zeros((128, 128), jnp.float32)
    for i in range(ROWS // 128):
        there = slice(i * 128, (i + 1) * 128)
        total = total + gibbs_ref[here, there] * scale_ref[:, there]
    return jnp.sum(total.T, axis=0, keepdims=True)


def column_kernel(gibbs_ref, parts_ref, mass_ref, part_ref, scale_ref):
    scale_ref[...] = mass_ref[...] / summed(parts_ref)
    for j in range(COLS // 128):
        total = columns(gibbs_ref, scale_ref, j)
        for k in range(NY):
            part_ref[k, :, j * 128 : (j + 1) * 128] = total


def relay_kernel(parts_ref, part_ref):
    total = summed(parts_ref)
    for k in range(part_ref.shape[0]):
        part_ref[k] = total


def last_column_kernel(gibbs_ref, parts_ref, mass_ref, leaving_ref, scale_ref):
    scale_ref[...] = mass_ref[...] / summed(parts_ref)
    me = lax.axis_index("x") * NC + lax.axis_index("core")
    own = scale_ref[:, pl.ds(pl.multiple_of(me * OWN, OWN), OWN)]
    for j in range(COLS // 128):
        total = columns(gibbs_ref, scale_ref, j)
        for k in (2 * j, 2 * j + 1):
            leaving_ref[k, :, 0:OWN] = own
            leaving_ref[k, :, OWN : OWN + 128] = total
            total = pltpu.roll(total, PIECE, 1)


def row_kernel(gibbs_ref, parts_ref, mass_ref, part_ref):
    scale = mass_ref[...] / summed(parts_ref)
    totals = [jnp.zeros((8, 128), jnp.float32)] * (ROWS // 128)
    for j in range(COLS // 128):
        here = slice(j * 128, (j + 1) * 128)
        spread = jnp.broadcast_to(scale[:, here], (128, 128)).T
        for i in range(ROWS // 128):
            there = slice(i * 128, (i + 1) * 128)
            totals[i] = totals[i] + jnp.sum((gibbs_ref[here, there] * spread).reshape(16, 8, 128), axis=0)
    for i in range(ROWS // 128):
        total = jnp.sum(totals[i], axis=0, keepdims=True)
        for k in range(NG):
            part_ref[k, :, i * 128 : (i + 1) * 128] = total


def landing_kernel(landed_ref, rows_ref, part_ref):
    total = jnp.zeros((1, 128), jnp.float32)
    for k in range(NZ):
        rows_ref[k] = EPS * jnp.log(landed_ref[k, :, 0:OWN])
        total = total + landed_ref[k, :, OWN : OWN + 128]
    for k in range(NY * NG):
        part_ref[k] = total


def potential_kernel(parts_ref, mass_ref, out_ref):
    lane = lax.broadcasted_iota(jnp.int32, (1, 128), 1)
    for t in range(NG // 2):
        a, b = (sum(parts_ref[y * NG + g] for y in range(NY)) for g in (2 * t, 2 * t + 1))
        total = jnp.where(lane < PIECE, a, pltpu.roll(b, PIECE, 1))
        out_ref[t : t + 1] = EPS * jnp.log(mass_ref[t : t + 1] / total)


def f32(*shape):
    return jax.ShapeDtypeStruct(shape, jnp.float32)


def call(kernel, outs, *args, scratch=()):
    whole = pl.BlockSpec(memory_space=pltpu.VMEM)
    return pl.pallas_call(
        kernel,
        out_shape=outs,
        in_specs=[whole] * len(args),
        out_specs=[whole] * len(outs),
        scratch_shapes=list(scratch),
        compiler_params=pltpu.CompilerParams(vmem_limit_bytes=24 << 20),
    )(*args)


def swap(value, axes):
    return lax.all_to_all(value, axes, 0, 0, tiled=True)


def local(src_cells, tgt_cells, src_mass, tgt_mass):
    tgt_mass = tgt_mass.reshape(NX, 128)
    rows, cols = call(
        pack_kernel, (f32(64, OWN), f32(NZ * HALF, 128)), src_cells, tgt_cells, src_mass.reshape(NZ * 2, 128), tgt_mass
    )
    cols = swap(cols.reshape(NZ, 1, HALF * 128), "z").reshape(NZ * HALF, 128)
    rows = lax.all_gather(rows, "core")
    others = [lax.ppermute(rows, "x", [(i, (i + k) % NX) for i in range(NX)]) for k in range(1, NX)]
    gibbs, row_parts, row_mass, col_mass = call(
        gibbs_kernel,
        (f32(COLS, ROWS), f32(NG, 1, ROWS), f32(1, ROWS), f32(1, COLS)),
        rows,
        *others,
        cols,
        scratch=(pltpu.VMEM((256, ROWS), jnp.bfloat16), pltpu.VMEM((COLS, 256), jnp.bfloat16)),
    )
    scale = pltpu.VMEM((1, ROWS), jnp.float32)
    (col_parts,) = call(
        column_kernel, (f32(NY, 1, COLS),), gibbs, swap(row_parts, GROUP), row_mass, scratch=(scale,)
    )
    (col_parts,) = call(relay_kernel, (f32(NZ, 1, COLS),), swap(col_parts, "y"))
    col_parts = swap(col_parts, "z")
    (row_parts,) = call(row_kernel, (f32(NG, 1, ROWS),), gibbs, col_parts, col_mass)
    (leaving,) = call(
        last_column_kernel, (f32(NZ, 1, OWN + 128),), gibbs, swap(row_parts, GROUP), row_mass, scratch=(scale,)
    )
    row_out, col_parts = call(landing_kernel, (f32(NZ, 1, OWN), f32(NY * NG, 1, 128)), swap(leaving, "z"))
    (col_out,) = call(potential_kernel, (f32(NX, 128),), swap(col_parts, PLANE), tgt_mass)
    return row_out.reshape(NZ * OWN), col_out.reshape(NX * 128)


def solution(mesh):
    grid = Mesh(mesh.devices.reshape(NY, NX, NC, NZ), ("y", "x", "core", "z"))
    placed = (P(None, PLANE + ("z",)), P(None, "z"), P(PLANE), P("z"))
    return jax.shard_map(local, mesh=grid, in_specs=placed, out_specs=(P(PLANE), P("z")), check_vma=False)
```

```python
import jax
import jax.numpy as jnp
from jax import lax
from jax.experimental import pallas as pl
from jax.experimental.pallas import tpu as pltpu
from jax.sharding import Mesh, PartitionSpec as P

NY, NX, NC, NZ = 4, 4, 2, 16
NG = NX * NC
PLANE = ("y", "x", "core")
GROUP = ("x", "core")
PC = 50
HALF = 26
MASS = 56
ROWS, COLS = 2048, 1024
PIECE = 64
OWN = 256
EPS = 2.0
FULL = 60 << 20


def split(value):
    high = value.astype(jnp.bfloat16)
    low = (value - high.astype(jnp.float32)).astype(jnp.bfloat16)
    return high, low


def pieces(norm):
    first = norm.astype(jnp.bfloat16).astype(jnp.float32)
    rest = norm - first
    second = rest.astype(jnp.bfloat16).astype(jnp.float32)
    return first, second, rest - second


def masked(cells):
    row = lax.broadcasted_iota(jnp.int32, cells.shape, 0)
    keep = (row < HALF) | ((row >= 32) & (row < 32 + PC - HALF))
    return row, jnp.where(keep, cells, 0.0)


def pack_kernel(tgt_ref, tgt_mass_ref, src_ref, src_mass_ref, cols_ref, rows_ref, tgt_buf, tgt_mass_buf, src_buf, src_mass_buf, sems):
    x, core, z = (lax.axis_index(name) for name in ("x", "core", "z"))
    here = pl.ds(pl.multiple_of(x * 128, 128), 128)
    copies = [
        pltpu.make_async_copy(source, target, sems.at[k])
        for k, (source, target) in enumerate(
            (
                (tgt_ref.at[:, here], tgt_buf),
                (tgt_mass_ref, tgt_mass_buf),
                (src_ref, src_buf),
                (src_mass_ref, src_mass_buf),
            )
        )
    ]
    for copy in copies:
        copy.start()
    rows_ref[...] = jnp.zeros_like(rows_ref)
    for copy in copies:
        copy.wait()
    rows_ref[0:HALF] = src_buf[0:HALF]
    rows_ref[32 : 32 + PC - HALF] = src_buf[HALF:PC]
    for k in range(2):
        rows_ref[MASS : MASS + 1, k * 128 : (k + 1) * 128] = src_mass_buf[pl.ds(2 * z + k, 1)]
    cells = tgt_buf[...]
    top = cells[0:HALF]
    bottom = jnp.concatenate([cells[HALF:PC], tgt_mass_buf[pl.ds(x, 1)], jnp.zeros((1, 128), jnp.float32)], axis=0)
    lane = lax.broadcasted_iota(jnp.int32, (HALF, 128), 1)
    first = jnp.where(lane < PIECE, top, pltpu.roll(bottom, PIECE, 1))
    second = jnp.where(lane < PIECE, pltpu.roll(top, PIECE, 1), bottom)
    piece = jnp.where(jnp.broadcast_to(core, (HALF, 128)) == 0, first, second)
    for k in range(NZ):
        cols_ref[k * HALF : (k + 1) * HALF] = piece


def stack_kernel(own_ref, one_ref, two_ref, three_ref, x_ref, row_mass_ref):
    x = lax.axis_index("x")
    for k, rows_ref in enumerate((own_ref, one_ref, two_ref, three_ref)):
        base = pl.multiple_of(lax.rem(x + NX - k, NX) * (NC * OWN), NC * OWN)
        for c in range(NC):
            here = pl.ds(pl.multiple_of(base + c * OWN, OWN), OWN)
            cells = rows_ref[c]
            row_mass_ref[:, here] = cells[MASS : MASS + 1]
            row, cells = masked(cells)
            first, second, third = pieces(-0.5 * jnp.sum(cells * cells, axis=0, keepdims=True))
            high, low = split(cells)
            extra = jnp.where(row == 26, first, jnp.where(row == 27, second, jnp.where(row == 28, third, 0.0)))
            extra = jnp.where((row >= 29) & (row < 32), 1.0, extra)
            x_ref[0:64, here] = (high.astype(jnp.float32) + extra).astype(jnp.bfloat16)
            x_ref[64:128, here] = high
            x_ref[128:192, here] = low
            x_ref[192:256, here] = low


def gibbs_kernel(x_ref, cols_ref, gibbs_ref, part_ref, col_mass_ref, y_ref):
    lane = lax.broadcasted_iota(jnp.int32, (32, 128), 1)
    gap = jnp.zeros((32 - HALF, 128), jnp.float32)
    for t in range(NZ // 2):
        here = slice(t * 128, (t + 1) * 128)
        a, b = (
            jnp.concatenate([cols_ref[k * HALF : (k + 1) * HALF], gap], axis=0) for k in (2 * t, 2 * t + 1)
        )
        top = jnp.where(lane < PIECE, a, pltpu.roll(b, PIECE, 1))
        bottom = jnp.where(lane < PIECE, pltpu.roll(a, PIECE, 1), b)
        col_mass_ref[:, here] = bottom[MASS - 32 : MASS - 31]
        row, cells = masked(jnp.concatenate([top, bottom], axis=0))
        first, second, third = pieces(-0.5 * jnp.sum(cells * cells, axis=0, keepdims=True))
        high, low = split(cells)
        extra = jnp.where(row == 29, first, jnp.where(row == 30, second, jnp.where(row == 31, third, 0.0)))
        extra = jnp.where((row >= 26) & (row < 29), 1.0, extra)
        both = jnp.concatenate([high.astype(jnp.float32) + extra, low.astype(jnp.float32)], axis=0)
        turned = both.T.astype(jnp.bfloat16)
        y_ref[here, 0:128] = turned
        y_ref[here, 128:256] = turned
    for n in range(ROWS // 256):
        there = slice(n * 256, (n + 1) * 256)
        total = jnp.zeros((8, 256), jnp.float32)
        for m in range(COLS // 256):
            here = slice(m * 256, (m + 1) * 256)
            tile = jnp.exp(jnp.dot(y_ref[here, :], x_ref[:, there], preferred_element_type=jnp.float32))
            gibbs_ref[here, there] = tile
            total = total + jnp.sum(tile.reshape(32, 8, 256), axis=0)
        total = jnp.sum(total, axis=0, keepdims=True)
        for k in range(NG):
            part_ref[k, :, there] = total


def summed(parts_ref):
    total = parts_ref[0]
    for k in range(1, parts_ref.shape[0]):
        total = total + parts_ref[k]
    return total


def columns(gibbs_ref, scale_ref, j):
    here = slice(j * 128, (j + 1) * 128)
    total = jnp.zeros((128, 128), jnp.float32)
    for i in range(ROWS // 128):
        there = slice(i * 128, (i + 1) * 128)
        total = total + gibbs_ref[here, there] * scale_ref[:, there]
    return jnp.sum(total.T, axis=0, keepdims=True)


def column_kernel(gibbs_ref, parts_ref, mass_ref, part_ref, scale_ref):
    scale_ref[...] = mass_ref[...] / summed(parts_ref)
    for j in range(COLS // 128):
        total = columns(gibbs_ref, scale_ref, j)
        for k in range(NY):
            part_ref[k, :, j * 128 : (j + 1) * 128] = total


def relay_kernel(parts_ref, part_ref):
    total = summed(parts_ref)
    for k in range(part_ref.shape[0]):
        part_ref[k] = total


def last_column_kernel(gibbs_ref, parts_ref, mass_ref, leaving_ref, scale_ref):
    scale_ref[...] = mass_ref[...] / summed(parts_ref)
    me = lax.axis_index("x") * NC + lax.axis_index("core")
    own = scale_ref[:, pl.ds(pl.multiple_of(me * OWN, OWN), OWN)]
    for j in range(COLS // 128):
        total = columns(gibbs_ref, scale_ref, j)
        for k in (2 * j, 2 * j + 1):
            leaving_ref[k, :, 0:OWN] = own
            leaving_ref[k, :, OWN : OWN + 128] = total
            total = pltpu.roll(total, PIECE, 1)


def row_kernel(gibbs_ref, parts_ref, mass_ref, part_ref):
    scale = mass_ref[...] / summed(parts_ref)
    totals = [jnp.zeros((8, 128), jnp.float32)] * (ROWS // 128)
    for j in range(COLS // 128):
        here = slice(j * 128, (j + 1) * 128)
        spread = jnp.broadcast_to(scale[:, here], (128, 128)).T
        for i in range(ROWS // 128):
            there = slice(i * 128, (i + 1) * 128)
            totals[i] = totals[i] + jnp.sum((gibbs_ref[here, there] * spread).reshape(16, 8, 128), axis=0)
    for i in range(ROWS // 128):
        total = jnp.sum(totals[i], axis=0, keepdims=True)
        for k in range(NG):
            part_ref[k, :, i * 128 : (i + 1) * 128] = total


def landing_kernel(landed_ref, part_ref):
    total = landed_ref[0, :, OWN : OWN + 128]
    for k in range(1, NZ):
        total = total + landed_ref[k, :, OWN : OWN + 128]
    for k in range(NY * NG):
        part_ref[k] = total


def potential_kernel(landed_ref, parts_ref, mass_ref, rows_ref, out_ref):
    for k in range(NZ):
        rows_ref[k] = EPS * jnp.log(landed_ref[k, :, 0:OWN])
    lane = lax.broadcasted_iota(jnp.int32, (1, 128), 1)
    for t in range(NG // 2):
        a, b = (sum(parts_ref[y * NG + g] for y in range(NY)) for g in (2 * t, 2 * t + 1))
        total = jnp.where(lane < PIECE, a, pltpu.roll(b, PIECE, 1))
        out_ref[t : t + 1] = EPS * jnp.log(mass_ref[t : t + 1] / total)


def f32(*shape):
    return jax.ShapeDtypeStruct(shape, jnp.float32)


def call(kernel, outs, *args, scratch=(), space=pltpu.VMEM, limit=24 << 20):
    whole = pl.BlockSpec(memory_space=pltpu.VMEM)
    return pl.pallas_call(
        kernel,
        out_shape=outs,
        in_specs=[pl.BlockSpec(memory_space=space)] * len(args),
        out_specs=[whole] * len(outs),
        scratch_shapes=list(scratch),
        compiler_params=pltpu.CompilerParams(vmem_limit_bytes=limit),
    )(*args)


def swap(value, axes):
    return lax.all_to_all(value, axes, 0, 0, tiled=True)


def local(src_cells, tgt_cells, src_mass, tgt_mass):
    tgt_mass = tgt_mass.reshape(NX, 128)
    cols, rows = call(
        pack_kernel,
        (f32(NZ * HALF, 128), f32(64, OWN)),
        tgt_cells,
        tgt_mass,
        src_cells,
        src_mass.reshape(NZ * 2, 128),
        scratch=[pltpu.VMEM(shape, jnp.float32) for shape in ((PC, 128), (NX, 128), (PC, OWN), (NZ * 2, 128))]
        + [pltpu.SemaphoreType.DMA((4,))],
        space=pltpu.HBM,
        limit=FULL,
    )
    cols = swap(cols.reshape(NZ, 1, HALF * 128), "z").reshape(NZ * HALF, 128)
    rows = lax.all_gather(rows, "core")
    others = [lax.ppermute(rows, "x", [(i, (i + k) % NX) for i in range(NX)]) for k in range(1, NX)]
    stack, row_mass = call(
        stack_kernel, (jax.ShapeDtypeStruct((256, ROWS), jnp.bfloat16), f32(1, ROWS)), rows, *others
    )
    gibbs, row_parts, col_mass = call(
        gibbs_kernel,
        (f32(COLS, ROWS), f32(NG, 1, ROWS), f32(1, COLS)),
        stack,
        cols,
        scratch=(pltpu.VMEM((COLS, 256), jnp.bfloat16),),
    )
    scale = pltpu.VMEM((1, ROWS), jnp.float32)
    (col_parts,) = call(
        column_kernel, (f32(NY, 1, COLS),), gibbs, swap(row_parts, GROUP), row_mass, scratch=(scale,)
    )
    (col_parts,) = call(relay_kernel, (f32(NZ, 1, COLS),), swap(col_parts, "y"))
    col_parts = swap(col_parts, "z")
    (row_parts,) = call(row_kernel, (f32(NG, 1, ROWS),), gibbs, col_parts, col_mass)
    (leaving,) = call(
        last_column_kernel, (f32(NZ, 1, OWN + 128),), gibbs, swap(row_parts, GROUP), row_mass, scratch=(scale,)
    )
    landed = swap(leaving, "z")
    (col_parts,) = call(landing_kernel, (f32(NY * NG, 1, 128),), landed)
    row_out, col_out = call(
        potential_kernel, (f32(NZ, 1, OWN), f32(NX, 128)), landed, swap(col_parts, PLANE), tgt_mass
    )
    return row_out.reshape(NZ * OWN), col_out.reshape(NX * 128)


def solution(mesh):
    grid = Mesh(mesh.devices.reshape(NY, NX, NC, NZ), ("y", "x", "core", "z"))
    placed = (P(None, PLANE + ("z",)), P(None, "z"), P(PLANE), P("z"))
    return jax.shard_map(local, mesh=grid, in_specs=placed, out_specs=(P(PLANE), P("z")), check_vma=False)
```

```python
import jax
import jax.numpy as jnp
from jax import lax
from jax.experimental import pallas as pl
from jax.experimental.pallas import tpu as pltpu
from jax.sharding import Mesh, PartitionSpec as P

NY, NH, NL, NC, NZ = 4, 2, 2, 2, 16
NX = NH * NL
NG = NL * NC
NS = NY * NH
PLANE = ("y", "half", "x", "core")
GROUP = ("x", "core")
PC = 50
STEP = 13
MASS = 59
QUARTER = 32
OWN = 256
ROWS, COLS = NG * OWN, NZ * 128
EPS = 2.0


def split(value):
    high = value.astype(jnp.bfloat16)
    low = (value - high.astype(jnp.float32)).astype(jnp.bfloat16)
    return high, low


def augmented(cells, norm_row, ones_row):
    row = lax.broadcasted_iota(jnp.int32, cells.shape, 0)
    keep = (lax.rem(row, 16) < STEP) & (row < MASS)
    cells = jnp.where(keep, cells, 0.0)
    norm = -0.5 * jnp.sum(cells * cells, axis=0, keepdims=True)
    first = norm.astype(jnp.bfloat16).astype(jnp.float32)
    rest = norm - first
    second = rest.astype(jnp.bfloat16).astype(jnp.float32)
    extra = jnp.where((row >= ones_row) & (row < ones_row + 3), 1.0, 0.0)
    for k, piece in enumerate((first, second, rest - second)):
        extra = jnp.where(row == norm_row + k, piece, extra)
    high, low = split(cells)
    return high, low, high.astype(jnp.float32) + extra


def pack_kernel(tgt_ref, tgt_mass_ref, src_ref, src_mass_ref, cols_ref, rows_ref, tgt_buf, tgt_mass_buf, src_buf, src_mass_buf, sems):
    y, x, core, z = (lax.axis_index(name) for name in ("y", "x", "core", "z"))
    me = x * NC + core
    here = pl.ds(pl.multiple_of(me * 128, 128), 128)
    pairs = (
        (tgt_ref.at[:, here], tgt_buf),
        (tgt_mass_ref, tgt_mass_buf),
        (src_ref, src_buf),
        (src_mass_ref, src_mass_buf),
    )
    copies = [pltpu.make_async_copy(a, b, sems.at[k]) for k, (a, b) in enumerate(pairs)]
    for copy in copies:
        copy.start()
    rows_ref[...] = jnp.zeros_like(rows_ref)
    for copy in copies:
        copy.wait()
    for q in range(4):
        rows_ref[16 * q : 16 * q + min(STEP, PC - STEP * q)] = src_buf[STEP * q : min(STEP * (q + 1), PC)]
    for k in range(2):
        rows_ref[MASS : MASS + 1, k * 128 : (k + 1) * 128] = src_mass_buf[pl.ds(2 * z + k, 1)]
    cells = jnp.concatenate([tgt_buf[...], tgt_mass_buf[pl.ds(me, 1)], jnp.zeros((5, 128), jnp.float32)], axis=0)
    cells = pltpu.roll(cells, lax.rem(128 - QUARTER * y, 128), 1)
    lane = lax.broadcasted_iota(jnp.int32, (STEP, 128), 1)
    piece = cells[0:STEP]
    for q in range(1, 4):
        moved = pltpu.roll(cells[STEP * q : STEP * (q + 1)], QUARTER * q, 1)
        piece = jnp.where(lane < QUARTER * q, piece, moved)
    for k in range(NZ):
        cols_ref[k * STEP : (k + 1) * STEP] = piece


def stack_kernel(rows_ref, x_ref, row_mass_ref):
    for g in range(NG):
        here = slice(g * OWN, (g + 1) * OWN)
        cells = rows_ref[g]
        row_mass_ref[:, here] = cells[MASS : MASS + 1]
        high, low, plus = augmented(cells, 13, 29)
        x_ref[0:64, here] = plus.astype(jnp.bfloat16)
        x_ref[64:128, here] = high
        x_ref[128:192, here] = low
        x_ref[192:256, here] = low


def copy_kernel(cols_ref, out_ref):
    value = cols_ref[...]
    for k in range(NY):
        out_ref[k] = value


def gibbs_kernel(x_ref, cols_ref, gibbs_ref, part_ref, col_mass_ref, y_ref):
    lane = lax.broadcasted_iota(jnp.int32, (16, 128), 1)
    gap = jnp.zeros((16 - STEP, 128), jnp.float32)
    for z in range(NZ):
        here = slice(z * 128, (z + 1) * 128)
        taken = [jnp.concatenate([cols_ref[y, z * STEP : (z + 1) * STEP], gap], axis=0) for y in range(NY)]
        groups = []
        for q in range(4):
            moved = [pltpu.roll(taken[y], QUARTER * (y - q) % 128, 1) if y != q else taken[y] for y in range(NY)]
            group = moved[0]
            for y in range(1, NY):
                group = jnp.where(lane < QUARTER * y, group, moved[y])
            groups.append(group)
        cells = jnp.concatenate(groups, axis=0)
        col_mass_ref[:, here] = cells[MASS : MASS + 1]
        high, low, plus = augmented(cells, 29, 13)
        turned = jnp.concatenate([plus, low.astype(jnp.float32)], axis=0).T.astype(jnp.bfloat16)
        y_ref[here, 0:128] = turned
        y_ref[here, 128:256] = turned
    for n in range(ROWS // 256):
        there = slice(n * 256, (n + 1) * 256)
        total = jnp.zeros((8, 256), jnp.float32)
        for m in range(COLS // 256):
            here = slice(m * 256, (m + 1) * 256)
            tile = jnp.exp(jnp.dot(y_ref[here, :], x_ref[:, there], preferred_element_type=jnp.float32))
            gibbs_ref[here, there] = tile
            total = total + jnp.sum(tile.reshape(32, 8, 256), axis=0)
        part_ref[:, there] = jnp.sum(total, axis=0, keepdims=True)


def summed(parts_ref):
    total = parts_ref[0]
    for k in range(1, parts_ref.shape[0]):
        total = total + parts_ref[k]
    return total


def columns(gibbs_ref, scale_ref, j):
    here = slice(j * 128, (j + 1) * 128)
    total = jnp.zeros((128, 128), jnp.float32)
    for i in range(ROWS // 128):
        there = slice(i * 128, (i + 1) * 128)
        total = total + gibbs_ref[here, there] * scale_ref[:, there]
    return jnp.sum(total.T, axis=0, keepdims=True)


def column_kernel(gibbs_ref, parts_ref, mass_ref, part_ref, scale_ref):
    scale_ref[...] = mass_ref[...] / summed(parts_ref)
    for j in range(COLS // 128):
        total = columns(gibbs_ref, scale_ref, j)
        for k in range(NS):
            part_ref[k, :, j * 128 : (j + 1) * 128] = total


def relay_kernel(parts_ref, part_ref):
    total = summed(parts_ref)
    for k in range(part_ref.shape[0]):
        part_ref[k] = total


def last_column_kernel(gibbs_ref, parts_ref, mass_ref, leaving_ref, scale_ref):
    scale_ref[...] = mass_ref[...] / summed(parts_ref)
    me = lax.axis_index("x") * NC + lax.axis_index("core")
    own = scale_ref[:, pl.ds(pl.multiple_of(me * OWN, OWN), OWN)]
    for j in range(NZ):
        leaving_ref[j, :, 0:OWN] = own
        leaving_ref[j, :, OWN : OWN + 128] = columns(gibbs_ref, scale_ref, j)


def row_kernel(gibbs_ref, parts_ref, mass_ref, part_ref):
    scale = mass_ref[...] / summed(parts_ref)
    totals = [jnp.zeros((8, 128), jnp.float32)] * (ROWS // 128)
    for j in range(COLS // 128):
        here = slice(j * 128, (j + 1) * 128)
        spread = jnp.broadcast_to(scale[:, here], (128, 128)).T
        for i in range(ROWS // 128):
            there = slice(i * 128, (i + 1) * 128)
            totals[i] = totals[i] + jnp.sum((gibbs_ref[here, there] * spread).reshape(16, 8, 128), axis=0)
    for i in range(ROWS // 128):
        part_ref[:, i * 128 : (i + 1) * 128] = jnp.sum(totals[i], axis=0, keepdims=True)


def landing_kernel(landed_ref, part_ref):
    total = landed_ref[0, :, OWN : OWN + 128]
    for k in range(1, NZ):
        total = total + landed_ref[k, :, OWN : OWN + 128]
    for k in range(NS * NG):
        part_ref[k] = total


def potential_kernel(landed_ref, parts_ref, mass_ref, rows_ref, out_ref):
    for k in range(NZ):
        rows_ref[k] = EPS * jnp.log(landed_ref[k, :, 0:OWN])
    for t in range(NG):
        total = parts_ref[t]
        for k in range(1, NS):
            total = total + parts_ref[k * NG + t]
        out_ref[t : t + 1] = EPS * jnp.log(mass_ref[t : t + 1] / total)


def f32(*shape):
    return jax.ShapeDtypeStruct(shape, jnp.float32)


def call(kernel, outs, *args, scratch=(), space=pltpu.VMEM, limit=24 << 20):
    whole = pl.BlockSpec(memory_space=pltpu.VMEM)
    return pl.pallas_call(
        kernel,
        out_shape=outs,
        in_specs=[pl.BlockSpec(memory_space=space)] * len(args),
        out_specs=[whole] * len(outs),
        scratch_shapes=list(scratch),
        compiler_params=pltpu.CompilerParams(vmem_limit_bytes=limit),
    )(*args)


def swap(value, axes):
    return lax.all_to_all(value, axes, 0, 0, tiled=True)


def local(src_cells, tgt_cells, src_mass, tgt_mass):
    tgt_mass = tgt_mass.reshape(NG, 128)
    cols, rows = call(
        pack_kernel,
        (f32(NZ * STEP, 128), f32(64, OWN)),
        tgt_cells,
        tgt_mass,
        src_cells,
        src_mass.reshape(NZ * 2, 128),
        scratch=[pltpu.VMEM(shape, jnp.float32) for shape in ((PC, 128), (NG, 128), (PC, OWN), (NZ * 2, 128))]
        + [pltpu.SemaphoreType.DMA((4,))],
        space=pltpu.HBM,
        limit=60 << 20,
    )
    cols = swap(cols.reshape(NZ, 1, STEP * 128), "z").reshape(NZ * STEP, 128)
    stack, row_mass = call(
        stack_kernel,
        (jax.ShapeDtypeStruct((256, ROWS), jnp.bfloat16), f32(1, ROWS)),
        lax.all_gather(rows, GROUP),
    )
    cols, stack = lax.optimization_barrier((cols, stack))
    (cols,) = call(copy_kernel, (f32(NY, NZ * STEP, 128),), cols)
    cols = swap(cols.reshape(NY, 1, NZ * STEP * 128), "y").reshape(NY, NZ * STEP, 128)
    gibbs, row_part, col_mass = call(
        gibbs_kernel,
        (f32(COLS, ROWS), f32(1, ROWS), f32(1, COLS)),
        stack,
        cols,
        scratch=(pltpu.VMEM((COLS, 256), jnp.bfloat16),),
    )
    scale = pltpu.VMEM((1, ROWS), jnp.float32)
    row_parts = lax.all_gather(row_part, GROUP)
    (col_parts,) = call(column_kernel, (f32(NS, 1, COLS),), gibbs, row_parts, row_mass, scratch=(scale,))
    (col_parts,) = call(relay_kernel, (f32(NZ, 1, COLS),), swap(col_parts, ("y", "half")))
    (row_part,) = call(row_kernel, (f32(1, ROWS),), gibbs, swap(col_parts, "z"), col_mass)
    row_parts = lax.all_gather(row_part, GROUP)
    (leaving,) = call(
        last_column_kernel, (f32(NZ, 1, OWN + 128),), gibbs, row_parts, row_mass, scratch=(scale,)
    )
    landed = swap(leaving, "z")
    (col_parts,) = call(landing_kernel, (f32(NS * NG, 1, 128),), landed)
    row_out, col_out = call(
        potential_kernel, (f32(NZ, 1, OWN), f32(NG, 128)), landed, swap(col_parts, PLANE), tgt_mass
    )
    return row_out.reshape(NZ * OWN), col_out.reshape(NG * 128)


def solution(mesh):
    grid = Mesh(mesh.devices.reshape(NY, NH, NL, NC, NZ), PLANE + ("z",))
    placed = (P(None, PLANE + ("z",)), P(None, "z"), P(PLANE), P("z"))
    return jax.shard_map(local, mesh=grid, in_specs=placed, out_specs=(P(PLANE), P("z")), check_vma=False)
```

```python
import jax
import jax.numpy as jnp
from jax import lax
from jax.experimental import pallas as pl
from jax.experimental.pallas import tpu as pltpu
from jax.sharding import Mesh, PartitionSpec as P

NY, NX, NC, NZ = 4, 4, 2, 16
NG = NX * NC
PLANE = ("y", "x", "core")
GROUP = ("x", "core")
PC = 50
HALF = 26
MASS = 56
ROWS, COLS = 2048, 1024
PIECE = 64
OWN = 256
EPS = 2.0
FULL = 60 << 20


def split(value):
    high = value.astype(jnp.bfloat16)
    low = (value - high.astype(jnp.float32)).astype(jnp.bfloat16)
    return high, low


def pieces(norm):
    first = norm.astype(jnp.bfloat16).astype(jnp.float32)
    rest = norm - first
    second = rest.astype(jnp.bfloat16).astype(jnp.float32)
    return first, second, rest - second


def masked(cells):
    row = lax.broadcasted_iota(jnp.int32, cells.shape, 0)
    keep = (row < HALF) | ((row >= 32) & (row < 32 + PC - HALF))
    return row, jnp.where(keep, cells, 0.0)


def pack_kernel(tgt_ref, tgt_mass_ref, cols_ref, cells_ref, mass_ref, sems):
    x, core = lax.axis_index("x"), lax.axis_index("core")
    here = pl.ds(pl.multiple_of(x * 128, 128), 128)
    copies = (
        pltpu.make_async_copy(tgt_ref.at[:, here], cells_ref, sems.at[0]),
        pltpu.make_async_copy(tgt_mass_ref, mass_ref, sems.at[1]),
    )
    for copy in copies:
        copy.start()
    for copy in copies:
        copy.wait()
    cells = cells_ref[...]
    top = cells[0:HALF]
    bottom = jnp.concatenate([cells[HALF:PC], mass_ref[pl.ds(x, 1)], jnp.zeros((1, 128), jnp.float32)], axis=0)
    lane = lax.broadcasted_iota(jnp.int32, (HALF, 128), 1)
    first = jnp.where(lane < PIECE, top, pltpu.roll(bottom, PIECE, 1))
    second = jnp.where(lane < PIECE, pltpu.roll(top, PIECE, 1), bottom)
    piece = jnp.where(jnp.broadcast_to(core, (HALF, 128)) == 0, first, second)
    for k in range(NZ):
        cols_ref[k * HALF : (k + 1) * HALF] = piece


def stack_kernel(rows_ref, mass_ref, x_ref, own_mass_ref):
    z = lax.axis_index("z")
    for k in range(2):
        own_mass_ref[:, k * 128 : (k + 1) * 128] = mass_ref[pl.ds(2 * z + k, 1)]
    for g in range(NG):
        here = slice(g * OWN, (g + 1) * OWN)
        cells = rows_ref[g]
        norm = -0.5 * jnp.sum(cells * cells, axis=0, keepdims=True)
        ones = jnp.ones((3, OWN), jnp.float32)
        high, low = split(cells)
        high = high.astype(jnp.float32)
        low = low.astype(jnp.float32)
        gap = jnp.zeros((8, OWN), jnp.float32)
        plus = jnp.concatenate([high[0:HALF], *pieces(norm), ones, high[HALF:PC], gap], axis=0)
        low = jnp.concatenate([low[0:HALF], gap[0:6], low[HALF:PC], gap], axis=0).astype(jnp.bfloat16)
        row = lax.broadcasted_iota(jnp.int32, (64, OWN), 0)
        x_ref[0:64, here] = plus.astype(jnp.bfloat16)
        x_ref[64:128, here] = jnp.where((row < HALF) | (row >= 32), plus, 0.0).astype(jnp.bfloat16)
        x_ref[128:192, here] = low
        x_ref[192:256, here] = low


def gibbs_kernel(x_ref, cols_ref, mass_ref, gibbs_ref, part_ref, col_mass_ref, y_ref):
    for k in range(NG):
        part_ref[k, :, ROWS : ROWS + OWN] = mass_ref[...]
    lane = lax.broadcasted_iota(jnp.int32, (32, 128), 1)
    gap = jnp.zeros((32 - HALF, 128), jnp.float32)
    for t in range(NZ // 2):
        here = slice(t * 128, (t + 1) * 128)
        a, b = (
            jnp.concatenate([cols_ref[k * HALF : (k + 1) * HALF], gap], axis=0) for k in (2 * t, 2 * t + 1)
        )
        top = jnp.where(lane < PIECE, a, pltpu.roll(b, PIECE, 1))
        bottom = jnp.where(lane < PIECE, pltpu.roll(a, PIECE, 1), b)
        col_mass_ref[:, here] = bottom[MASS - 32 : MASS - 31]
        row, cells = masked(jnp.concatenate([top, bottom], axis=0))
        first, second, third = pieces(-0.5 * jnp.sum(cells * cells, axis=0, keepdims=True))
        high, low = split(cells)
        extra = jnp.where(row == 29, first, jnp.where(row == 30, second, jnp.where(row == 31, third, 0.0)))
        extra = jnp.where((row >= 26) & (row < 29), 1.0, extra)
        both = jnp.concatenate([high.astype(jnp.float32) + extra, low.astype(jnp.float32)], axis=0)
        turned = both.T.astype(jnp.bfloat16)
        y_ref[here, 0:128] = turned
        y_ref[here, 128:256] = turned
    for n in range(ROWS // 256):
        there = slice(n * 256, (n + 1) * 256)
        total = jnp.zeros((8, 256), jnp.float32)
        for m in range(COLS // 256):
            here = slice(m * 256, (m + 1) * 256)
            tile = jnp.exp(jnp.dot(y_ref[here, :], x_ref[:, there], preferred_element_type=jnp.float32))
            gibbs_ref[here, there] = tile
            total = total + jnp.sum(tile.reshape(32, 8, 256), axis=0)
        total = jnp.sum(total, axis=0, keepdims=True)
        for k in range(NG):
            part_ref[k, :, there] = total


def summed(parts_ref):
    total = parts_ref[0]
    for k in range(1, parts_ref.shape[0]):
        total = total + parts_ref[k]
    return total


def columns(gibbs_ref, scale_ref, j):
    here = slice(j * 128, (j + 1) * 128)
    total = jnp.zeros((128, 128), jnp.float32)
    for i in range(ROWS // 128):
        there = slice(i * 128, (i + 1) * 128)
        total = total + gibbs_ref[here, there] * scale_ref[:, there]
    return jnp.sum(total.T, axis=0, keepdims=True)


def column_kernel(gibbs_ref, parts_ref, part_ref, mass_ref, scale_ref):
    for k in range(NG):
        mass_ref[:, k * OWN : (k + 1) * OWN] = parts_ref[k, :, ROWS : ROWS + OWN]
    total = parts_ref[0, :, 0:ROWS]
    for k in range(1, NG):
        total = total + parts_ref[k, :, 0:ROWS]
    scale_ref[...] = mass_ref[...] / total
    for j in range(COLS // 128):
        total = columns(gibbs_ref, scale_ref, j)
        for k in range(NY):
            part_ref[k, :, j * 128 : (j + 1) * 128] = total


def relay_kernel(parts_ref, part_ref):
    total = summed(parts_ref)
    for k in range(part_ref.shape[0]):
        part_ref[k] = total


def last_column_kernel(gibbs_ref, parts_ref, mass_ref, leaving_ref, scale_ref):
    scale_ref[...] = mass_ref[...] / summed(parts_ref)
    me = lax.axis_index("x") * NC + lax.axis_index("core")
    own = scale_ref[:, pl.ds(pl.multiple_of(me * OWN, OWN), OWN)]
    for j in range(COLS // 128):
        total = columns(gibbs_ref, scale_ref, j)
        for k in (2 * j, 2 * j + 1):
            leaving_ref[k, :, 0:OWN] = own
            leaving_ref[k, :, OWN : OWN + 128] = total
            total = pltpu.roll(total, PIECE, 1)


def row_kernel(gibbs_ref, parts_ref, mass_ref, part_ref):
    scale = mass_ref[...] / summed(parts_ref)
    totals = [jnp.zeros((8, 128), jnp.float32)] * (ROWS // 128)
    for j in range(COLS // 128):
        here = slice(j * 128, (j + 1) * 128)
        spread = jnp.broadcast_to(scale[:, here], (128, 128)).T
        for i in range(ROWS // 128):
            there = slice(i * 128, (i + 1) * 128)
            totals[i] = totals[i] + jnp.sum((gibbs_ref[here, there] * spread).reshape(16, 8, 128), axis=0)
    for i in range(ROWS // 128):
        total = jnp.sum(totals[i], axis=0, keepdims=True)
        for k in range(NG):
            part_ref[k, :, i * 128 : (i + 1) * 128] = total


def landing_kernel(landed_ref, part_ref):
    total = landed_ref[0, :, OWN : OWN + 128]
    for k in range(1, NZ):
        total = total + landed_ref[k, :, OWN : OWN + 128]
    for k in range(NY * NG):
        part_ref[k] = total


def potential_kernel(landed_ref, parts_ref, mass_ref, rows_ref, out_ref):
    for k in range(NZ):
        rows_ref[k] = EPS * jnp.log(landed_ref[k, :, 0:OWN])
    lane = lax.broadcasted_iota(jnp.int32, (1, 128), 1)
    for t in range(NG // 2):
        a, b = (sum(parts_ref[y * NG + g] for y in range(NY)) for g in (2 * t, 2 * t + 1))
        total = jnp.where(lane < PIECE, a, pltpu.roll(b, PIECE, 1))
        out_ref[t : t + 1] = EPS * jnp.log(mass_ref[t : t + 1] / total)


def f32(*shape):
    return jax.ShapeDtypeStruct(shape, jnp.float32)


def call(kernel, outs, *args, scratch=(), space=pltpu.VMEM, limit=24 << 20):
    whole = pl.BlockSpec(memory_space=pltpu.VMEM)
    return pl.pallas_call(
        kernel,
        out_shape=outs,
        in_specs=[pl.BlockSpec(memory_space=space)] * len(args),
        out_specs=[whole] * len(outs),
        scratch_shapes=list(scratch),
        compiler_params=pltpu.CompilerParams(vmem_limit_bytes=limit),
    )(*args)


def swap(value, axes):
    return lax.all_to_all(value, axes, 0, 0, tiled=True)


def local(src_cells, tgt_cells, src_mass, tgt_mass):
    tgt_mass = tgt_mass.reshape(NX, 128)
    (cols,) = call(
        pack_kernel,
        (f32(NZ * HALF, 128),),
        tgt_cells,
        tgt_mass,
        scratch=[pltpu.VMEM((PC, 128), jnp.float32), pltpu.VMEM((NX, 128), jnp.float32), pltpu.SemaphoreType.DMA((2,))],
        space=pltpu.HBM,
        limit=60 << 20,
    )
    cols = swap(cols.reshape(NZ, 1, HALF * 128), "z").reshape(NZ * HALF, 128)
    stack, own_mass = call(
        stack_kernel,
        (jax.ShapeDtypeStruct((256, ROWS), jnp.bfloat16), f32(1, OWN)),
        lax.all_gather(src_cells, GROUP),
        src_mass.reshape(NZ * 2, 128),
    )
    gibbs, row_parts, col_mass = call(
        gibbs_kernel,
        (f32(COLS, ROWS), f32(NG, 1, ROWS + OWN), f32(1, COLS)),
        stack,
        cols,
        own_mass,
        scratch=(pltpu.VMEM((COLS, 256), jnp.bfloat16),),
    )
    scale = pltpu.VMEM((1, ROWS), jnp.float32)
    col_parts, row_mass = call(
        column_kernel, (f32(NY, 1, COLS), f32(1, ROWS)), gibbs, swap(row_parts, GROUP), scratch=(scale,)
    )
    (col_parts,) = call(relay_kernel, (f32(NZ, 1, COLS),), swap(col_parts, "y"))
    col_parts = swap(col_parts, "z")
    (row_parts,) = call(row_kernel, (f32(NG, 1, ROWS),), gibbs, col_parts, col_mass)
    (leaving,) = call(
        last_column_kernel, (f32(NZ, 1, OWN + 128),), gibbs, swap(row_parts, GROUP), row_mass, scratch=(scale,)
    )
    landed = swap(leaving, "z")
    (col_parts,) = call(landing_kernel, (f32(NY * NG, 1, 128),), landed)
    row_out, col_out = call(
        potential_kernel, (f32(NZ, 1, OWN), f32(NX, 128)), landed, swap(col_parts, PLANE), tgt_mass
    )
    return row_out.reshape(NZ * OWN), col_out.reshape(NX * 128)


def solution(mesh):
    grid = Mesh(mesh.devices.reshape(NY, NX, NC, NZ), ("y", "x", "core", "z"))
    placed = (P(None, PLANE + ("z",)), P(None, "z"), P(PLANE), P("z"))
    return jax.shard_map(local, mesh=grid, in_specs=placed, out_specs=(P(PLANE), P("z")), check_vma=False)
```

```python
import jax
import jax.numpy as jnp
from jax import lax
from jax.experimental import pallas as pl
from jax.experimental.pallas import tpu as pltpu
from jax.sharding import Mesh, PartitionSpec as P

NY, NX, NC, NZ = 4, 4, 2, 16
NG = NX * NC
PLANE = ("y", "x", "core")
GROUP = ("x", "core")
PC = 50
HALF = 26
MASS = 56
ROWS, COLS = 2048, 1024
PIECE = 64
OWN = 256
ORDER = [(8 - k) % NZ for k in range(NZ)]
EPS = 2.0
FULL = 60 << 20


def split(value):
    high = value.astype(jnp.bfloat16)
    low = (value - high.astype(jnp.float32)).astype(jnp.bfloat16)
    return high, low


def pieces(norm):
    first = norm.astype(jnp.bfloat16).astype(jnp.float32)
    rest = norm - first
    second = rest.astype(jnp.bfloat16).astype(jnp.float32)
    return first, second, rest - second


def masked(cells):
    row = lax.broadcasted_iota(jnp.int32, cells.shape, 0)
    keep = (row < HALF) | ((row >= 32) & (row < 32 + PC - HALF))
    return row, jnp.where(keep, cells, 0.0)


def pack_kernel(tgt_ref, tgt_mass_ref, cols_ref, cells_ref, mass_ref, sems):
    x, core = lax.axis_index("x"), lax.axis_index("core")
    here = pl.ds(pl.multiple_of(x * 128, 128), 128)
    copies = (
        pltpu.make_async_copy(tgt_ref.at[:, here], cells_ref, sems.at[0]),
        pltpu.make_async_copy(tgt_mass_ref, mass_ref, sems.at[1]),
    )
    for copy in copies:
        copy.start()
    for copy in copies:
        copy.wait()
    cells = cells_ref[...]
    top = cells[0:HALF]
    bottom = jnp.concatenate([cells[HALF:PC], mass_ref[pl.ds(x, 1)], jnp.zeros((1, 128), jnp.float32)], axis=0)
    lane = lax.broadcasted_iota(jnp.int32, (HALF, 128), 1)
    first = jnp.where(lane < PIECE, top, pltpu.roll(bottom, PIECE, 1))
    second = jnp.where(lane < PIECE, pltpu.roll(top, PIECE, 1), bottom)
    piece = jnp.where(jnp.broadcast_to(core, (HALF, 128)) == 0, first, second)
    for k in range(NZ):
        cols_ref[k * HALF : (k + 1) * HALF] = piece


def stack_kernel(rows_ref, mass_ref, x_ref, own_mass_ref):
    z = lax.axis_index("z")
    for k in range(2):
        own_mass_ref[:, k * 128 : (k + 1) * 128] = mass_ref[pl.ds(2 * z + k, 1)]
    for g in range(NG):
        here = slice(g * OWN, (g + 1) * OWN)
        cells = rows_ref[g]
        norm = -0.5 * jnp.sum(cells * cells, axis=0, keepdims=True)
        ones = jnp.ones((3, OWN), jnp.float32)
        high, low = split(cells)
        high = high.astype(jnp.float32)
        low = low.astype(jnp.float32)
        gap = jnp.zeros((8, OWN), jnp.float32)
        plus = jnp.concatenate([high[0:HALF], *pieces(norm), ones, high[HALF:PC], gap], axis=0)
        low = jnp.concatenate([low[0:HALF], gap[0:6], low[HALF:PC], gap], axis=0).astype(jnp.bfloat16)
        row = lax.broadcasted_iota(jnp.int32, (64, OWN), 0)
        x_ref[0:64, here] = plus.astype(jnp.bfloat16)
        x_ref[64:128, here] = jnp.where((row < HALF) | (row >= 32), plus, 0.0).astype(jnp.bfloat16)
        x_ref[128:192, here] = low
        x_ref[192:256, here] = low


def gibbs_kernel(x_ref, cols_ref, mass_ref, gibbs_ref, part_ref, col_mass_ref, y_ref):
    for k in range(NG):
        part_ref[k, :, ROWS : ROWS + OWN] = mass_ref[...]
    lane = lax.broadcasted_iota(jnp.int32, (32, 128), 1)
    gap = jnp.zeros((32 - HALF, 128), jnp.float32)
    for t in range(NZ // 2):
        here = slice(t * 128, (t + 1) * 128)
        a, b = (
            jnp.concatenate([cols_ref[k * HALF : (k + 1) * HALF], gap], axis=0) for k in (2 * t, 2 * t + 1)
        )
        top = jnp.where(lane < PIECE, a, pltpu.roll(b, PIECE, 1))
        bottom = jnp.where(lane < PIECE, pltpu.roll(a, PIECE, 1), b)
        col_mass_ref[:, here] = bottom[MASS - 32 : MASS - 31]
        row, cells = masked(jnp.concatenate([top, bottom], axis=0))
        first, second, third = pieces(-0.5 * jnp.sum(cells * cells, axis=0, keepdims=True))
        high, low = split(cells)
        extra = jnp.where(row == 29, first, jnp.where(row == 30, second, jnp.where(row == 31, third, 0.0)))
        extra = jnp.where((row >= 26) & (row < 29), 1.0, extra)
        both = jnp.concatenate([high.astype(jnp.float32) + extra, low.astype(jnp.float32)], axis=0)
        turned = both.T.astype(jnp.bfloat16)
        y_ref[here, 0:128] = turned
        y_ref[here, 128:256] = turned
    for n in range(ROWS // 256):
        there = slice(n * 256, (n + 1) * 256)
        total = jnp.zeros((8, 256), jnp.float32)
        for m in range(COLS // 256):
            here = slice(m * 256, (m + 1) * 256)
            tile = jnp.exp(jnp.dot(y_ref[here, :], x_ref[:, there], preferred_element_type=jnp.float32))
            gibbs_ref[here, there] = tile
            total = total + jnp.sum(tile.reshape(32, 8, 256), axis=0)
        total = jnp.sum(total, axis=0, keepdims=True)
        for k in range(NG):
            part_ref[k, :, there] = total


def summed(parts_ref):
    total = parts_ref[0]
    for k in range(1, parts_ref.shape[0]):
        total = total + parts_ref[k]
    return total


def columns(gibbs_ref, scale_ref, j):
    here = slice(j * 128, (j + 1) * 128)
    total = jnp.zeros((128, 128), jnp.float32)
    for i in range(ROWS // 128):
        there = slice(i * 128, (i + 1) * 128)
        total = total + gibbs_ref[here, there] * scale_ref[:, there]
    return jnp.sum(total.T, axis=0, keepdims=True)


def column_kernel(gibbs_ref, parts_ref, part_ref, mass_ref, scale_ref):
    for k in range(NG):
        mass_ref[:, k * OWN : (k + 1) * OWN] = parts_ref[k, :, ROWS : ROWS + OWN]
    total = parts_ref[0, :, 0:ROWS]
    for k in range(1, NG):
        total = total + parts_ref[k, :, 0:ROWS]
    scale_ref[...] = mass_ref[...] / total
    for j in range(COLS // 128):
        total = columns(gibbs_ref, scale_ref, j)
        for k in range(NY):
            part_ref[k, :, j * 128 : (j + 1) * 128] = total


def relay_kernel(parts_ref, part_ref):
    total = summed(parts_ref)
    for k in range(part_ref.shape[0]):
        part_ref[k] = total


def last_column_kernel(gibbs_ref, parts_ref, mass_ref, leaving_ref, scale_ref):
    scale_ref[...] = mass_ref[...] / summed(parts_ref)
    me = lax.axis_index("x") * NC + lax.axis_index("core")
    own = scale_ref[:, pl.ds(pl.multiple_of(me * OWN, OWN), OWN)]
    for j in range(COLS // 128):
        total = columns(gibbs_ref, scale_ref, j)
        for k in (ORDER[2 * j], ORDER[2 * j + 1]):
            leaving_ref[k, :, 0:OWN] = own
            leaving_ref[k, :, OWN : OWN + 128] = total
            total = pltpu.roll(total, PIECE, 1)


def row_kernel(gibbs_ref, parts_ref, mass_ref, part_ref):
    scale = mass_ref[...] / summed(parts_ref)
    totals = [jnp.zeros((8, 128), jnp.float32)] * (ROWS // 128)
    for j in range(COLS // 128):
        here = slice(j * 128, (j + 1) * 128)
        spread = jnp.broadcast_to(scale[:, here], (128, 128)).T
        for i in range(ROWS // 128):
            there = slice(i * 128, (i + 1) * 128)
            totals[i] = totals[i] + jnp.sum((gibbs_ref[here, there] * spread).reshape(16, 8, 128), axis=0)
    for i in range(ROWS // 128):
        total = jnp.sum(totals[i], axis=0, keepdims=True)
        for k in range(NG):
            part_ref[k, :, i * 128 : (i + 1) * 128] = total


def landing_kernel(landed_ref, part_ref):
    total = landed_ref[0, :, OWN : OWN + 128]
    for k in range(1, NZ):
        total = total + landed_ref[k, :, OWN : OWN + 128]
    for k in range(NY * NG):
        part_ref[k] = total


def potential_kernel(landed_ref, parts_ref, mass_ref, rows_ref, out_ref):
    for k in range(NZ):
        rows_ref[k] = EPS * jnp.log(landed_ref[k, :, 0:OWN])
    lane = lax.broadcasted_iota(jnp.int32, (1, 128), 1)
    for t in range(NG // 2):
        a, b = (sum(parts_ref[y * NG + g] for y in range(NY)) for g in (2 * t, 2 * t + 1))
        total = jnp.where(lane < PIECE, a, pltpu.roll(b, PIECE, 1))
        out_ref[t : t + 1] = EPS * jnp.log(mass_ref[t : t + 1] / total)


def f32(*shape):
    return jax.ShapeDtypeStruct(shape, jnp.float32)


def call(kernel, outs, *args, scratch=(), space=pltpu.VMEM, limit=24 << 20):
    whole = pl.BlockSpec(memory_space=pltpu.VMEM)
    return pl.pallas_call(
        kernel,
        out_shape=outs,
        in_specs=[pl.BlockSpec(memory_space=space)] * len(args),
        out_specs=[whole] * len(outs),
        scratch_shapes=list(scratch),
        compiler_params=pltpu.CompilerParams(vmem_limit_bytes=limit),
    )(*args)


def swap(value, axes, groups=None):
    return lax.all_to_all(value, axes, 0, 0, tiled=True, axis_index_groups=groups)


def local(src_cells, tgt_cells, src_mass, tgt_mass):
    tgt_mass = tgt_mass.reshape(NX, 128)
    (cols,) = call(
        pack_kernel,
        (f32(NZ * HALF, 128),),
        tgt_cells,
        tgt_mass,
        scratch=[pltpu.VMEM((PC, 128), jnp.float32), pltpu.VMEM((NX, 128), jnp.float32), pltpu.SemaphoreType.DMA((2,))],
        space=pltpu.HBM,
        limit=60 << 20,
    )
    cols = swap(cols.reshape(NZ, 1, HALF * 128), "z", [ORDER]).reshape(NZ * HALF, 128)
    stack, own_mass = call(
        stack_kernel,
        (jax.ShapeDtypeStruct((256, ROWS), jnp.bfloat16), f32(1, OWN)),
        lax.all_gather(src_cells, GROUP),
        src_mass.reshape(NZ * 2, 128),
    )
    gibbs, row_parts, col_mass = call(
        gibbs_kernel,
        (f32(COLS, ROWS), f32(NG, 1, ROWS + OWN), f32(1, COLS)),
        stack,
        cols,
        own_mass,
        scratch=(pltpu.VMEM((COLS, 256), jnp.bfloat16),),
    )
    scale = pltpu.VMEM((1, ROWS), jnp.float32)
    col_parts, row_mass = call(
        column_kernel, (f32(NY, 1, COLS), f32(1, ROWS)), gibbs, swap(row_parts, GROUP), scratch=(scale,)
    )
    (col_parts,) = call(relay_kernel, (f32(NZ, 1, COLS),), swap(col_parts, "y"))
    col_parts = swap(col_parts, "z")
    (row_parts,) = call(row_kernel, (f32(NG, 1, ROWS),), gibbs, col_parts, col_mass)
    (leaving,) = call(
        last_column_kernel, (f32(NZ, 1, OWN + 128),), gibbs, swap(row_parts, GROUP), row_mass, scratch=(scale,)
    )
    landed = swap(leaving, "z")
    (col_parts,) = call(landing_kernel, (f32(NY * NG, 1, 128),), landed)
    row_out, col_out = call(
        potential_kernel, (f32(NZ, 1, OWN), f32(NX, 128)), landed, swap(col_parts, PLANE), tgt_mass
    )
    return row_out.reshape(NZ * OWN), col_out.reshape(NX * 128)


def solution(mesh):
    grid = Mesh(mesh.devices.reshape(NY, NX, NC, NZ), ("y", "x", "core", "z"))
    placed = (P(None, PLANE + ("z",)), P(None, "z"), P(PLANE), P("z"))
    return jax.shard_map(local, mesh=grid, in_specs=placed, out_specs=(P(PLANE), P("z")), check_vma=False)
```

```python
import jax
import jax.numpy as jnp
from jax import lax
from jax.experimental import pallas as pl
from jax.experimental.pallas import tpu as pltpu
from jax.sharding import Mesh, PartitionSpec as P

NY, NX, NC, NZ = 4, 4, 2, 16
NG = NX * NC
PLANE = ("y", "x", "core")
GROUP = ("x", "core")
PC = 50
HALF = 26
MASS = 56
ROWS, COLS = 2048, 1024
PIECE = 64
OWN = 256
ORDER = [(12 - k) % NZ for k in range(NZ)]
EPS = 2.0
FULL = 60 << 20


def split(value):
    high = value.astype(jnp.bfloat16)
    low = (value - high.astype(jnp.float32)).astype(jnp.bfloat16)
    return high, low


def pieces(norm):
    first = norm.astype(jnp.bfloat16).astype(jnp.float32)
    rest = norm - first
    second = rest.astype(jnp.bfloat16).astype(jnp.float32)
    return first, second, rest - second


def masked(cells):
    row = lax.broadcasted_iota(jnp.int32, cells.shape, 0)
    keep = (row < HALF) | ((row >= 32) & (row < 32 + PC - HALF))
    return row, jnp.where(keep, cells, 0.0)


def pack_kernel(tgt_ref, tgt_mass_ref, cols_ref, cells_ref, mass_ref, sems):
    x, core = lax.axis_index("x"), lax.axis_index("core")
    here = pl.ds(pl.multiple_of(x * 128, 128), 128)
    copies = (
        pltpu.make_async_copy(tgt_ref.at[:, here], cells_ref, sems.at[0]),
        pltpu.make_async_copy(tgt_mass_ref, mass_ref, sems.at[1]),
    )
    for copy in copies:
        copy.start()
    for copy in copies:
        copy.wait()
    cells = cells_ref[...]
    top = cells[0:HALF]
    bottom = jnp.concatenate([cells[HALF:PC], mass_ref[pl.ds(x, 1)], jnp.zeros((1, 128), jnp.float32)], axis=0)
    lane = lax.broadcasted_iota(jnp.int32, (HALF, 128), 1)
    first = jnp.where(lane < PIECE, top, pltpu.roll(bottom, PIECE, 1))
    second = jnp.where(lane < PIECE, pltpu.roll(top, PIECE, 1), bottom)
    piece = jnp.where(jnp.broadcast_to(core, (HALF, 128)) == 0, first, second)
    for k in range(NZ):
        cols_ref[k * HALF : (k + 1) * HALF] = piece


def stack_kernel(rows_ref, mass_ref, x_ref, own_mass_ref):
    z = lax.axis_index("z")
    for k in range(2):
        own_mass_ref[:, k * 128 : (k + 1) * 128] = mass_ref[pl.ds(2 * z + k, 1)]
    for g in range(NG):
        here = slice(g * OWN, (g + 1) * OWN)
        cells = rows_ref[g]
        norm = -0.5 * jnp.sum(cells * cells, axis=0, keepdims=True)
        ones = jnp.ones((3, OWN), jnp.float32)
        high, low = split(cells)
        high = high.astype(jnp.float32)
        low = low.astype(jnp.float32)
        gap = jnp.zeros((8, OWN), jnp.float32)
        plus = jnp.concatenate([high[0:HALF], *pieces(norm), ones, high[HALF:PC], gap], axis=0)
        low = jnp.concatenate([low[0:HALF], gap[0:6], low[HALF:PC], gap], axis=0).astype(jnp.bfloat16)
        row = lax.broadcasted_iota(jnp.int32, (64, OWN), 0)
        x_ref[0:64, here] = plus.astype(jnp.bfloat16)
        x_ref[64:128, here] = jnp.where((row < HALF) | (row >= 32), plus, 0.0).astype(jnp.bfloat16)
        x_ref[128:192, here] = low
        x_ref[192:256, here] = low


def gibbs_kernel(x_ref, cols_ref, mass_ref, gibbs_ref, part_ref, col_mass_ref, y_ref):
    for k in range(NG):
        part_ref[k, :, ROWS : ROWS + OWN] = mass_ref[...]
    lane = lax.broadcasted_iota(jnp.int32, (32, 128), 1)
    gap = jnp.zeros((32 - HALF, 128), jnp.float32)
    for t in range(NZ // 2):
        here = slice(t * 128, (t + 1) * 128)
        a, b = (
            jnp.concatenate([cols_ref[k * HALF : (k + 1) * HALF], gap], axis=0) for k in (2 * t, 2 * t + 1)
        )
        top = jnp.where(lane < PIECE, a, pltpu.roll(b, PIECE, 1))
        bottom = jnp.where(lane < PIECE, pltpu.roll(a, PIECE, 1), b)
        col_mass_ref[:, here] = bottom[MASS - 32 : MASS - 31]
        row, cells = masked(jnp.concatenate([top, bottom], axis=0))
        first, second, third = pieces(-0.5 * jnp.sum(cells * cells, axis=0, keepdims=True))
        high, low = split(cells)
        extra = jnp.where(row == 29, first, jnp.where(row == 30, second, jnp.where(row == 31, third, 0.0)))
        extra = jnp.where((row >= 26) & (row < 29), 1.0, extra)
        both = jnp.concatenate([high.astype(jnp.float32) + extra, low.astype(jnp.float32)], axis=0)
        turned = both.T.astype(jnp.bfloat16)
        y_ref[here, 0:128] = turned
        y_ref[here, 128:256] = turned
    for n in range(ROWS // 256):
        there = slice(n * 256, (n + 1) * 256)
        total = jnp.zeros((8, 256), jnp.float32)
        for m in range(COLS // 256):
            here = slice(m * 256, (m + 1) * 256)
            tile = jnp.exp(jnp.dot(y_ref[here, :], x_ref[:, there], preferred_element_type=jnp.float32))
            gibbs_ref[here, there] = tile
            total = total + jnp.sum(tile.reshape(32, 8, 256), axis=0)
        total = jnp.sum(total, axis=0, keepdims=True)
        for k in range(NG):
            part_ref[k, :, there] = total


def summed(parts_ref):
    total = parts_ref[0]
    for k in range(1, parts_ref.shape[0]):
        total = total + parts_ref[k]
    return total


def columns(gibbs_ref, scale_ref, j):
    here = slice(j * 128, (j + 1) * 128)
    total = jnp.zeros((128, 128), jnp.float32)
    for i in range(ROWS // 128):
        there = slice(i * 128, (i + 1) * 128)
        total = total + gibbs_ref[here, there] * scale_ref[:, there]
    return jnp.sum(total.T, axis=0, keepdims=True)


def column_kernel(gibbs_ref, parts_ref, part_ref, mass_ref, scale_ref):
    for k in range(NG):
        mass_ref[:, k * OWN : (k + 1) * OWN] = parts_ref[k, :, ROWS : ROWS + OWN]
    total = parts_ref[0, :, 0:ROWS]
    for k in range(1, NG):
        total = total + parts_ref[k, :, 0:ROWS]
    scale_ref[...] = mass_ref[...] / total
    for j in range(COLS // 128):
        total = columns(gibbs_ref, scale_ref, j)
        for k in range(NY):
            part_ref[k, :, j * 128 : (j + 1) * 128] = total


def relay_kernel(parts_ref, part_ref):
    total = summed(parts_ref)
    for k in range(part_ref.shape[0]):
        part_ref[k] = total


def last_column_kernel(gibbs_ref, parts_ref, mass_ref, leaving_ref, scale_ref):
    scale_ref[...] = mass_ref[...] / summed(parts_ref)
    me = lax.axis_index("x") * NC + lax.axis_index("core")
    own = scale_ref[:, pl.ds(pl.multiple_of(me * OWN, OWN), OWN)]
    for j in range(COLS // 128):
        total = columns(gibbs_ref, scale_ref, j)
        for k in (ORDER[2 * j], ORDER[2 * j + 1]):
            leaving_ref[k, :, 0:OWN] = own
            leaving_ref[k, :, OWN : OWN + 128] = total
            total = pltpu.roll(total, PIECE, 1)


def row_kernel(gibbs_ref, parts_ref, mass_ref, part_ref):
    scale = mass_ref[...] / summed(parts_ref)
    totals = [jnp.zeros((8, 128), jnp.float32)] * (ROWS // 128)
    for j in range(COLS // 128):
        here = slice(j * 128, (j + 1) * 128)
        spread = jnp.broadcast_to(scale[:, here], (128, 128)).T
        for i in range(ROWS // 128):
            there = slice(i * 128, (i + 1) * 128)
            totals[i] = totals[i] + jnp.sum((gibbs_ref[here, there] * spread).reshape(16, 8, 128), axis=0)
    for i in range(ROWS // 128):
        total = jnp.sum(totals[i], axis=0, keepdims=True)
        for k in range(NG):
            part_ref[k, :, i * 128 : (i + 1) * 128] = total


def landing_kernel(landed_ref, part_ref):
    total = landed_ref[0, :, OWN : OWN + 128]
    for k in range(1, NZ):
        total = total + landed_ref[k, :, OWN : OWN + 128]
    for k in range(NY * NG):
        part_ref[k] = total


def potential_kernel(landed_ref, parts_ref, mass_ref, rows_ref, out_ref):
    for k in range(NZ):
        rows_ref[k] = EPS * jnp.log(landed_ref[k, :, 0:OWN])
    lane = lax.broadcasted_iota(jnp.int32, (1, 128), 1)
    for t in range(NG // 2):
        a, b = (sum(parts_ref[y * NG + g] for y in range(NY)) for g in (2 * t, 2 * t + 1))
        total = jnp.where(lane < PIECE, a, pltpu.roll(b, PIECE, 1))
        out_ref[t : t + 1] = EPS * jnp.log(mass_ref[t : t + 1] / total)


def f32(*shape):
    return jax.ShapeDtypeStruct(shape, jnp.float32)


def call(kernel, outs, *args, scratch=(), space=pltpu.VMEM, limit=24 << 20):
    whole = pl.BlockSpec(memory_space=pltpu.VMEM)
    return pl.pallas_call(
        kernel,
        out_shape=outs,
        in_specs=[pl.BlockSpec(memory_space=space)] * len(args),
        out_specs=[whole] * len(outs),
        scratch_shapes=list(scratch),
        compiler_params=pltpu.CompilerParams(vmem_limit_bytes=limit),
    )(*args)


def swap(value, axes, groups=None):
    return lax.all_to_all(value, axes, 0, 0, tiled=True, axis_index_groups=groups)


def local(src_cells, tgt_cells, src_mass, tgt_mass):
    tgt_mass = tgt_mass.reshape(NX, 128)
    (cols,) = call(
        pack_kernel,
        (f32(NZ * HALF, 128),),
        tgt_cells,
        tgt_mass,
        scratch=[pltpu.VMEM((PC, 128), jnp.float32), pltpu.VMEM((NX, 128), jnp.float32), pltpu.SemaphoreType.DMA((2,))],
        space=pltpu.HBM,
        limit=60 << 20,
    )
    cols = swap(cols.reshape(NZ, 1, HALF * 128), "z", [ORDER]).reshape(NZ * HALF, 128)
    stack, own_mass = call(
        stack_kernel,
        (jax.ShapeDtypeStruct((256, ROWS), jnp.bfloat16), f32(1, OWN)),
        lax.all_gather(src_cells, GROUP),
        src_mass.reshape(NZ * 2, 128),
    )
    gibbs, row_parts, col_mass = call(
        gibbs_kernel,
        (f32(COLS, ROWS), f32(NG, 1, ROWS + OWN), f32(1, COLS)),
        stack,
        cols,
        own_mass,
        scratch=(pltpu.VMEM((COLS, 256), jnp.bfloat16),),
    )
    scale = pltpu.VMEM((1, ROWS), jnp.float32)
    col_parts, row_mass = call(
        column_kernel, (f32(NY, 1, COLS), f32(1, ROWS)), gibbs, swap(row_parts, GROUP), scratch=(scale,)
    )
    (col_parts,) = call(relay_kernel, (f32(NZ, 1, COLS),), swap(col_parts, "y"))
    col_parts = swap(col_parts, "z")
    (row_parts,) = call(row_kernel, (f32(NG, 1, ROWS),), gibbs, col_parts, col_mass)
    (leaving,) = call(
        last_column_kernel, (f32(NZ, 1, OWN + 128),), gibbs, swap(row_parts, GROUP), row_mass, scratch=(scale,)
    )
    landed = swap(leaving, "z")
    (col_parts,) = call(landing_kernel, (f32(NY * NG, 1, 128),), landed)
    row_out, col_out = call(
        potential_kernel, (f32(NZ, 1, OWN), f32(NX, 128)), landed, swap(col_parts, PLANE), tgt_mass
    )
    return row_out.reshape(NZ * OWN), col_out.reshape(NX * 128)


def solution(mesh):
    grid = Mesh(mesh.devices.reshape(NY, NX, NC, NZ), ("y", "x", "core", "z"))
    placed = (P(None, PLANE + ("z",)), P(None, "z"), P(PLANE), P("z"))
    return jax.shard_map(local, mesh=grid, in_specs=placed, out_specs=(P(PLANE), P("z")), check_vma=False)
```

```python
import jax
import jax.numpy as jnp
from jax import lax
from jax.experimental import pallas as pl
from jax.experimental.pallas import tpu as pltpu
from jax.sharding import Mesh, PartitionSpec as P

NY, NX, NC, NZ = 4, 4, 2, 16
NG = NX * NC
PLANE = ("y", "x", "core")
GROUP = ("x", "core")
PC = 50
HALF = 26
MASS = 56
ROWS, COLS = 2048, 1024
PIECE = 64
OWN = 256
ORDER = [(12 + 7 * k) % NZ for k in range(NZ)]
EPS = 2.0
FULL = 60 << 20


def split(value):
    high = value.astype(jnp.bfloat16)
    low = (value - high.astype(jnp.float32)).astype(jnp.bfloat16)
    return high, low


def pieces(norm):
    first = norm.astype(jnp.bfloat16).astype(jnp.float32)
    rest = norm - first
    second = rest.astype(jnp.bfloat16).astype(jnp.float32)
    return first, second, rest - second


def masked(cells):
    row = lax.broadcasted_iota(jnp.int32, cells.shape, 0)
    keep = (row < HALF) | ((row >= 32) & (row < 32 + PC - HALF))
    return row, jnp.where(keep, cells, 0.0)


def pack_kernel(tgt_ref, tgt_mass_ref, src_ref, src_mass_ref, cols_ref, rows_ref, cells_ref, mass_ref, src_buf, src_mass_buf, sems):
    x, core, z = (lax.axis_index(name) for name in ("x", "core", "z"))
    here = pl.ds(pl.multiple_of(x * 128, 128), 128)
    copies = (
        pltpu.make_async_copy(tgt_ref.at[:, here], cells_ref, sems.at[0]),
        pltpu.make_async_copy(tgt_mass_ref, mass_ref, sems.at[1]),
        pltpu.make_async_copy(src_ref, src_buf, sems.at[2]),
        pltpu.make_async_copy(src_mass_ref, src_mass_buf, sems.at[3]),
    )
    for copy in copies:
        copy.start()
    for copy in copies:
        copy.wait()
    rows_ref[0:PC] = src_buf[...]
    for k in range(2):
        rows_ref[PC : PC + 1, k * 128 : (k + 1) * 128] = src_mass_buf[pl.ds(2 * z + k, 1)]
    cells = cells_ref[...]
    top = cells[0:HALF]
    bottom = jnp.concatenate([cells[HALF:PC], mass_ref[pl.ds(x, 1)], jnp.zeros((1, 128), jnp.float32)], axis=0)
    lane = lax.broadcasted_iota(jnp.int32, (HALF, 128), 1)
    first = jnp.where(lane < PIECE, top, pltpu.roll(bottom, PIECE, 1))
    second = jnp.where(lane < PIECE, pltpu.roll(top, PIECE, 1), bottom)
    piece = jnp.where(jnp.broadcast_to(core, (HALF, 128)) == 0, first, second)
    for k in range(NZ):
        cols_ref[k * HALF : (k + 1) * HALF] = piece


def stack_kernel(rows_ref, x_ref, row_mass_ref):
    for g in range(NG):
        here = slice(g * OWN, (g + 1) * OWN)
        row_mass_ref[:, here] = rows_ref[g, PC : PC + 1]
        cells = rows_ref[g, 0:PC]
        norm = -0.5 * jnp.sum(cells * cells, axis=0, keepdims=True)
        ones = jnp.ones((3, OWN), jnp.float32)
        high, low = split(cells)
        high = high.astype(jnp.float32)
        low = low.astype(jnp.float32)
        gap = jnp.zeros((8, OWN), jnp.float32)
        plus = jnp.concatenate([high[0:HALF], *pieces(norm), ones, high[HALF:PC], gap], axis=0)
        low = jnp.concatenate([low[0:HALF], gap[0:6], low[HALF:PC], gap], axis=0).astype(jnp.bfloat16)
        row = lax.broadcasted_iota(jnp.int32, (64, OWN), 0)
        x_ref[0:64, here] = plus.astype(jnp.bfloat16)
        x_ref[64:128, here] = jnp.where((row < HALF) | (row >= 32), plus, 0.0).astype(jnp.bfloat16)
        x_ref[128:192, here] = low
        x_ref[192:256, here] = low


def gibbs_kernel(x_ref, cols_ref, gibbs_ref, part_ref, col_mass_ref, y_ref):
    lane = lax.broadcasted_iota(jnp.int32, (32, 128), 1)
    gap = jnp.zeros((32 - HALF, 128), jnp.float32)
    for t in range(NZ // 2):
        here = slice(t * 128, (t + 1) * 128)
        a, b = (
            jnp.concatenate([cols_ref[k * HALF : (k + 1) * HALF], gap], axis=0) for k in (2 * t, 2 * t + 1)
        )
        top = jnp.where(lane < PIECE, a, pltpu.roll(b, PIECE, 1))
        bottom = jnp.where(lane < PIECE, pltpu.roll(a, PIECE, 1), b)
        col_mass_ref[:, here] = bottom[MASS - 32 : MASS - 31]
        row, cells = masked(jnp.concatenate([top, bottom], axis=0))
        first, second, third = pieces(-0.5 * jnp.sum(cells * cells, axis=0, keepdims=True))
        high, low = split(cells)
        extra = jnp.where(row == 29, first, jnp.where(row == 30, second, jnp.where(row == 31, third, 0.0)))
        extra = jnp.where((row >= 26) & (row < 29), 1.0, extra)
        both = jnp.concatenate([high.astype(jnp.float32) + extra, low.astype(jnp.float32)], axis=0)
        turned = both.T.astype(jnp.bfloat16)
        y_ref[here, 0:128] = turned
        y_ref[here, 128:256] = turned
    for n in range(ROWS // 256):
        there = slice(n * 256, (n + 1) * 256)
        total = jnp.zeros((8, 256), jnp.float32)
        for m in range(COLS // 256):
            here = slice(m * 256, (m + 1) * 256)
            tile = jnp.exp(jnp.dot(y_ref[here, :], x_ref[:, there], preferred_element_type=jnp.float32))
            gibbs_ref[here, there] = tile
            total = total + jnp.sum(tile.reshape(32, 8, 256), axis=0)
        total = jnp.sum(total, axis=0, keepdims=True)
        for k in range(NG):
            part_ref[k, :, there] = total


def summed(parts_ref):
    total = parts_ref[0]
    for k in range(1, parts_ref.shape[0]):
        total = total + parts_ref[k]
    return total


def columns(gibbs_ref, scale_ref, j):
    here = slice(j * 128, (j + 1) * 128)
    total = jnp.zeros((128, 128), jnp.float32)
    for i in range(ROWS // 128):
        there = slice(i * 128, (i + 1) * 128)
        total = total + gibbs_ref[here, there] * scale_ref[:, there]
    return jnp.sum(total.T, axis=0, keepdims=True)


def column_kernel(gibbs_ref, parts_ref, mass_ref, part_ref, scale_ref):
    scale_ref[...] = mass_ref[...] / summed(parts_ref)
    for j in range(COLS // 128):
        total = columns(gibbs_ref, scale_ref, j)
        for k in range(NY):
            part_ref[k, :, j * 128 : (j + 1) * 128] = total


def relay_kernel(parts_ref, part_ref):
    total = summed(parts_ref)
    for k in range(part_ref.shape[0]):
        part_ref[k] = total


def last_column_kernel(gibbs_ref, parts_ref, mass_ref, leaving_ref, scale_ref):
    scale_ref[...] = mass_ref[...] / summed(parts_ref)
    me = lax.axis_index("x") * NC + lax.axis_index("core")
    own = scale_ref[:, pl.ds(pl.multiple_of(me * OWN, OWN), OWN)]
    for j in range(COLS // 128):
        total = columns(gibbs_ref, scale_ref, j)
        for k in (ORDER[2 * j], ORDER[2 * j + 1]):
            leaving_ref[k, :, 0:OWN] = own
            leaving_ref[k, :, OWN : OWN + 128] = total
            total = pltpu.roll(total, PIECE, 1)


def row_kernel(gibbs_ref, parts_ref, mass_ref, part_ref):
    scale = mass_ref[...] / summed(parts_ref)
    totals = [jnp.zeros((8, 128), jnp.float32)] * (ROWS // 128)
    for j in range(COLS // 128):
        here = slice(j * 128, (j + 1) * 128)
        spread = jnp.broadcast_to(scale[:, here], (128, 128)).T
        for i in range(ROWS // 128):
            there = slice(i * 128, (i + 1) * 128)
            totals[i] = totals[i] + jnp.sum((gibbs_ref[here, there] * spread).reshape(16, 8, 128), axis=0)
    for i in range(ROWS // 128):
        total = jnp.sum(totals[i], axis=0, keepdims=True)
        for k in range(NG):
            part_ref[k, :, i * 128 : (i + 1) * 128] = total


def landing_kernel(landed_ref, part_ref):
    total = landed_ref[0, :, OWN : OWN + 128]
    for k in range(1, NZ):
        total = total + landed_ref[k, :, OWN : OWN + 128]
    for k in range(NY * NG):
        part_ref[k] = total


def potential_kernel(landed_ref, parts_ref, mass_ref, rows_ref, out_ref):
    for k in range(NZ):
        rows_ref[k] = EPS * jnp.log(landed_ref[k, :, 0:OWN])
    lane = lax.broadcasted_iota(jnp.int32, (1, 128), 1)
    for t in range(NG // 2):
        a, b = (sum(parts_ref[y * NG + g] for y in range(NY)) for g in (2 * t, 2 * t + 1))
        total = jnp.where(lane < PIECE, a, pltpu.roll(b, PIECE, 1))
        out_ref[t : t + 1] = EPS * jnp.log(mass_ref[t : t + 1] / total)


def f32(*shape):
    return jax.ShapeDtypeStruct(shape, jnp.float32)


def call(kernel, outs, *args, scratch=(), space=pltpu.VMEM, limit=24 << 20):
    whole = pl.BlockSpec(memory_space=pltpu.VMEM)
    return pl.pallas_call(
        kernel,
        out_shape=outs,
        in_specs=[pl.BlockSpec(memory_space=space)] * len(args),
        out_specs=[whole] * len(outs),
        scratch_shapes=list(scratch),
        compiler_params=pltpu.CompilerParams(vmem_limit_bytes=limit),
    )(*args)


def swap(value, axes, groups=None):
    return lax.all_to_all(value, axes, 0, 0, tiled=True, axis_index_groups=groups)


def local(src_cells, tgt_cells, src_mass, tgt_mass):
    tgt_mass = tgt_mass.reshape(NX, 128)
    cols, rows = call(
        pack_kernel,
        (f32(NZ * HALF, 128), f32(PC + 1, OWN)),
        tgt_cells,
        tgt_mass,
        src_cells,
        src_mass.reshape(NZ * 2, 128),
        scratch=[pltpu.VMEM(shape, jnp.float32) for shape in ((PC, 128), (NX, 128), (PC, OWN), (NZ * 2, 128))]
        + [pltpu.SemaphoreType.DMA((4,))],
        space=pltpu.HBM,
        limit=60 << 20,
    )
    cols = swap(cols.reshape(NZ, 1, HALF * 128), "z", [ORDER]).reshape(NZ * HALF, 128)
    stack, row_mass = call(
        stack_kernel,
        (jax.ShapeDtypeStruct((256, ROWS), jnp.bfloat16), f32(1, ROWS)),
        lax.all_gather(rows, GROUP),
    )
    gibbs, row_parts, col_mass = call(
        gibbs_kernel,
        (f32(COLS, ROWS), f32(NG, 1, ROWS), f32(1, COLS)),
        stack,
        cols,
        scratch=(pltpu.VMEM((COLS, 256), jnp.bfloat16),),
    )
    scale = pltpu.VMEM((1, ROWS), jnp.float32)
    (col_parts,) = call(
        column_kernel, (f32(NY, 1, COLS),), gibbs, swap(row_parts, GROUP), row_mass, scratch=(scale,)
    )
    (col_parts,) = call(relay_kernel, (f32(NZ, 1, COLS),), swap(col_parts, "y"))
    col_parts = swap(col_parts, "z")
    (row_parts,) = call(row_kernel, (f32(NG, 1, ROWS),), gibbs, col_parts, col_mass)
    (leaving,) = call(
        last_column_kernel, (f32(NZ, 1, OWN + 128),), gibbs, swap(row_parts, GROUP), row_mass, scratch=(scale,)
    )
    landed = swap(leaving, "z")
    (col_parts,) = call(landing_kernel, (f32(NY * NG, 1, 128),), landed)
    row_out, col_out = call(
        potential_kernel, (f32(NZ, 1, OWN), f32(NX, 128)), landed, swap(col_parts, PLANE), tgt_mass
    )
    return row_out.reshape(NZ * OWN), col_out.reshape(NX * 128)


def solution(mesh):
    grid = Mesh(mesh.devices.reshape(NY, NX, NC, NZ), ("y", "x", "core", "z"))
    placed = (P(None, PLANE + ("z",)), P(None, "z"), P(PLANE), P("z"))
    return jax.shard_map(local, mesh=grid, in_specs=placed, out_specs=(P(PLANE), P("z")), check_vma=False)
```

```python
import jax
import jax.numpy as jnp
from jax import lax
from jax.experimental import pallas as pl
from jax.experimental.pallas import tpu as pltpu
from jax.sharding import Mesh, PartitionSpec as P

NY, NX, NC, NZ = 4, 4, 2, 16
NG = NX * NC
PLANE = ("y", "x", "core")
GROUP = ("x", "core")
PC = 50
HALF = 26
MASS = 56
ROWS, COLS = 2048, 1024
PIECE = 64
OWN = 256
ORDER = [(12 - k) % NZ for k in range(NZ)]
EPS = 2.0
FULL = 60 << 20


def pieces(norm):
    first = norm.astype(jnp.bfloat16).astype(jnp.float32)
    rest = norm - first
    second = rest.astype(jnp.bfloat16).astype(jnp.float32)
    return first, second, rest - second


def masked(cells):
    row = lax.broadcasted_iota(jnp.int32, cells.shape, 0)
    keep = (row < HALF) | ((row >= 32) & (row < 32 + PC - HALF))
    return row, jnp.where(keep, cells, 0.0)


def pack_kernel(tgt_ref, tgt_mass_ref, cols_ref, cells_ref, mass_ref, sems):
    x, core = lax.axis_index("x"), lax.axis_index("core")
    here = pl.ds(pl.multiple_of(x * 128, 128), 128)
    copies = (
        pltpu.make_async_copy(tgt_ref.at[:, here], cells_ref, sems.at[0]),
        pltpu.make_async_copy(tgt_mass_ref, mass_ref, sems.at[1]),
    )
    for copy in copies:
        copy.start()
    for copy in copies:
        copy.wait()
    cells = cells_ref[...]
    top = cells[0:HALF]
    bottom = jnp.concatenate([cells[HALF:PC], mass_ref[pl.ds(x, 1)], jnp.zeros((1, 128), jnp.float32)], axis=0)
    lane = lax.broadcasted_iota(jnp.int32, (HALF, 128), 1)
    first = jnp.where(lane < PIECE, top, pltpu.roll(bottom, PIECE, 1))
    second = jnp.where(lane < PIECE, pltpu.roll(top, PIECE, 1), bottom)
    piece = jnp.where(jnp.broadcast_to(core, (HALF, 128)) == 0, first, second)
    for k in range(NZ):
        cols_ref[k * HALF : (k + 1) * HALF] = piece


def stack_kernel(rows_ref, mass_ref, x_ref, own_mass_ref):
    z = lax.axis_index("z")
    for k in range(2):
        own_mass_ref[:, k * 128 : (k + 1) * 128] = mass_ref[pl.ds(2 * z + k, 1)]
    for g in range(NG):
        here = slice(g * OWN, (g + 1) * OWN)
        cells = rows_ref[g]
        norm = -0.5 * jnp.sum(cells * cells, axis=0, keepdims=True)
        ones = jnp.ones((3, OWN), jnp.float32)
        high, mid, low = pieces(cells)
        gap = jnp.zeros((8, OWN), jnp.float32)
        plus = jnp.concatenate([high[0:HALF], *pieces(norm), ones, high[HALF:PC], gap], axis=0)
        row = lax.broadcasted_iota(jnp.int32, (64, OWN), 0)
        high = jnp.where((row < HALF) | (row >= 32), plus, 0.0).astype(jnp.bfloat16)
        mid, low = (
            jnp.concatenate([part[0:HALF], gap[0:6], part[HALF:PC], gap], axis=0).astype(jnp.bfloat16)
            for part in (mid, low)
        )
        for k, part in enumerate((plus.astype(jnp.bfloat16), high, mid, mid, high, low)):
            x_ref[64 * k : 64 * (k + 1), here] = part


def gibbs_kernel(x_ref, cols_ref, mass_ref, gibbs_ref, part_ref, col_mass_ref, y_ref):
    for k in range(NG):
        part_ref[k, :, ROWS : ROWS + OWN] = mass_ref[...]
    lane = lax.broadcasted_iota(jnp.int32, (32, 128), 1)
    gap = jnp.zeros((32 - HALF, 128), jnp.float32)
    for t in range(NZ // 2):
        here = slice(t * 128, (t + 1) * 128)
        a, b = (
            jnp.concatenate([cols_ref[k * HALF : (k + 1) * HALF], gap], axis=0) for k in (2 * t, 2 * t + 1)
        )
        top = jnp.where(lane < PIECE, a, pltpu.roll(b, PIECE, 1))
        bottom = jnp.where(lane < PIECE, pltpu.roll(a, PIECE, 1), b)
        col_mass_ref[:, here] = bottom[MASS - 32 : MASS - 31]
        row, cells = masked(jnp.concatenate([top, bottom], axis=0))
        first, second, third = pieces(-0.5 * jnp.sum(cells * cells, axis=0, keepdims=True))
        high, mid, low = pieces(cells)
        extra = jnp.where(row == 29, first, jnp.where(row == 30, second, jnp.where(row == 31, third, 0.0)))
        extra = jnp.where((row >= 26) & (row < 29), 1.0, extra)
        turned = jnp.concatenate([high + extra, mid], axis=0).T.astype(jnp.bfloat16)
        y_ref[here, 0:128] = turned
        y_ref[here, 128:256] = turned
        y_ref[here, 256:384] = jnp.concatenate([low, high], axis=0).T.astype(jnp.bfloat16)
    for n in range(ROWS // 256):
        there = slice(n * 256, (n + 1) * 256)
        total = jnp.zeros((8, 256), jnp.float32)
        for m in range(COLS // 256):
            here = slice(m * 256, (m + 1) * 256)
            tile = jnp.exp(jnp.dot(y_ref[here, :], x_ref[:, there], preferred_element_type=jnp.float32))
            gibbs_ref[here, there] = tile
            total = total + jnp.sum(tile.reshape(32, 8, 256), axis=0)
        total = jnp.sum(total, axis=0, keepdims=True)
        for k in range(NG):
            part_ref[k, :, there] = total


def summed(parts_ref):
    total = parts_ref[0]
    for k in range(1, parts_ref.shape[0]):
        total = total + parts_ref[k]
    return total


def columns(gibbs_ref, scale_ref, j):
    here = slice(j * 128, (j + 1) * 128)
    total = jnp.zeros((128, 128), jnp.float32)
    for i in range(ROWS // 128):
        there = slice(i * 128, (i + 1) * 128)
        total = total + gibbs_ref[here, there] * scale_ref[:, there]
    return jnp.sum(total.T, axis=0, keepdims=True)


def column_kernel(gibbs_ref, parts_ref, part_ref, mass_ref, scale_ref):
    for k in range(NG):
        mass_ref[:, k * OWN : (k + 1) * OWN] = parts_ref[k, :, ROWS : ROWS + OWN]
    total = parts_ref[0, :, 0:ROWS]
    for k in range(1, NG):
        total = total + parts_ref[k, :, 0:ROWS]
    scale_ref[...] = mass_ref[...] / total
    for j in range(COLS // 128):
        total = columns(gibbs_ref, scale_ref, j)
        for k in range(NY):
            part_ref[k, :, j * 128 : (j + 1) * 128] = total


def relay_kernel(parts_ref, part_ref):
    total = summed(parts_ref)
    for k in range(part_ref.shape[0]):
        part_ref[k] = total


def last_column_kernel(gibbs_ref, parts_ref, mass_ref, leaving_ref, scale_ref):
    scale_ref[...] = mass_ref[...] / summed(parts_ref)
    me = lax.axis_index("x") * NC + lax.axis_index("core")
    own = scale_ref[:, pl.ds(pl.multiple_of(me * OWN, OWN), OWN)]
    for j in range(COLS // 128):
        total = columns(gibbs_ref, scale_ref, j)
        for k in (ORDER[2 * j], ORDER[2 * j + 1]):
            leaving_ref[k, :, 0:OWN] = own
            leaving_ref[k, :, OWN : OWN + 128] = total
            total = pltpu.roll(total, PIECE, 1)


def row_kernel(gibbs_ref, parts_ref, mass_ref, part_ref):
    scale = mass_ref[...] / summed(parts_ref)
    totals = [jnp.zeros((8, 128), jnp.float32)] * (ROWS // 128)
    for j in range(COLS // 128):
        here = slice(j * 128, (j + 1) * 128)
        spread = jnp.broadcast_to(scale[:, here], (128, 128)).T
        for i in range(ROWS // 128):
            there = slice(i * 128, (i + 1) * 128)
            totals[i] = totals[i] + jnp.sum((gibbs_ref[here, there] * spread).reshape(16, 8, 128), axis=0)
    for i in range(ROWS // 128):
        total = jnp.sum(totals[i], axis=0, keepdims=True)
        for k in range(NG):
            part_ref[k, :, i * 128 : (i + 1) * 128] = total


def landing_kernel(landed_ref, part_ref):
    total = landed_ref[0, :, OWN : OWN + 128]
    for k in range(1, NZ):
        total = total + landed_ref[k, :, OWN : OWN + 128]
    for k in range(NY * NG):
        part_ref[k] = total


def potential_kernel(landed_ref, parts_ref, mass_ref, rows_ref, out_ref):
    for k in range(NZ):
        rows_ref[k] = EPS * jnp.log(landed_ref[k, :, 0:OWN])
    lane = lax.broadcasted_iota(jnp.int32, (1, 128), 1)
    for t in range(NG // 2):
        a, b = (sum(parts_ref[y * NG + g] for y in range(NY)) for g in (2 * t, 2 * t + 1))
        total = jnp.where(lane < PIECE, a, pltpu.roll(b, PIECE, 1))
        out_ref[t : t + 1] = EPS * jnp.log(mass_ref[t : t + 1] / total)


def f32(*shape):
    return jax.ShapeDtypeStruct(shape, jnp.float32)


def call(kernel, outs, *args, scratch=(), space=pltpu.VMEM, limit=24 << 20):
    whole = pl.BlockSpec(memory_space=pltpu.VMEM)
    return pl.pallas_call(
        kernel,
        out_shape=outs,
        in_specs=[pl.BlockSpec(memory_space=space)] * len(args),
        out_specs=[whole] * len(outs),
        scratch_shapes=list(scratch),
        compiler_params=pltpu.CompilerParams(vmem_limit_bytes=limit),
    )(*args)


def swap(value, axes, groups=None):
    return lax.all_to_all(value, axes, 0, 0, tiled=True, axis_index_groups=groups)


def local(src_cells, tgt_cells, src_mass, tgt_mass):
    tgt_mass = tgt_mass.reshape(NX, 128)
    (cols,) = call(
        pack_kernel,
        (f32(NZ * HALF, 128),),
        tgt_cells,
        tgt_mass,
        scratch=[pltpu.VMEM((PC, 128), jnp.float32), pltpu.VMEM((NX, 128), jnp.float32), pltpu.SemaphoreType.DMA((2,))],
        space=pltpu.HBM,
        limit=60 << 20,
    )
    cols = swap(cols.reshape(NZ, 1, HALF * 128), "z", [ORDER]).reshape(NZ * HALF, 128)
    stack, own_mass = call(
        stack_kernel,
        (jax.ShapeDtypeStruct((384, ROWS), jnp.bfloat16), f32(1, OWN)),
        lax.all_gather(src_cells, GROUP),
        src_mass.reshape(NZ * 2, 128),
    )
    gibbs, row_parts, col_mass = call(
        gibbs_kernel,
        (f32(COLS, ROWS), f32(NG, 1, ROWS + OWN), f32(1, COLS)),
        stack,
        cols,
        own_mass,
        scratch=(pltpu.VMEM((COLS, 384), jnp.bfloat16),),
    )
    scale = pltpu.VMEM((1, ROWS), jnp.float32)
    col_parts, row_mass = call(
        column_kernel, (f32(NY, 1, COLS), f32(1, ROWS)), gibbs, swap(row_parts, GROUP), scratch=(scale,)
    )
    (col_parts,) = call(relay_kernel, (f32(NZ, 1, COLS),), swap(col_parts, "y"))
    col_parts = swap(col_parts, "z")
    (row_parts,) = call(row_kernel, (f32(NG, 1, ROWS),), gibbs, col_parts, col_mass)
    (leaving,) = call(
        last_column_kernel, (f32(NZ, 1, OWN + 128),), gibbs, swap(row_parts, GROUP), row_mass, scratch=(scale,)
    )
    landed = swap(leaving, "z")
    (col_parts,) = call(landing_kernel, (f32(NY * NG, 1, 128),), landed)
    row_out, col_out = call(
        potential_kernel, (f32(NZ, 1, OWN), f32(NX, 128)), landed, swap(col_parts, PLANE), tgt_mass
    )
    return row_out.reshape(NZ * OWN), col_out.reshape(NX * 128)


def solution(mesh):
    grid = Mesh(mesh.devices.reshape(NY, NX, NC, NZ), ("y", "x", "core", "z"))
    placed = (P(None, PLANE + ("z",)), P(None, "z"), P(PLANE), P("z"))
    return jax.shard_map(local, mesh=grid, in_specs=placed, out_specs=(P(PLANE), P("z")), check_vma=False)
```

```python
import jax
import jax.numpy as jnp
from jax import lax
from jax.experimental import pallas as pl
from jax.experimental.pallas import tpu as pltpu
from jax.sharding import Mesh, PartitionSpec as P

NY, NX, NC, NZ = 4, 4, 2, 16
NG = NX * NC
PLANE = ("y", "x", "core")
GROUP = ("x", "core")
PC = 50
HALF = 26
MASS = 56
ROWS, COLS = 2048, 1024
PIECE = 64
OWN = 256
DOWN = [-k % NZ for k in range(NZ)]
ORDER = [(12 - k) % NZ for k in range(NZ)]
EPS = 2.0
FULL = 60 << 20


def pieces(norm):
    first = norm.astype(jnp.bfloat16).astype(jnp.float32)
    rest = norm - first
    second = rest.astype(jnp.bfloat16).astype(jnp.float32)
    return first, second, rest - second


def masked(cells):
    row = lax.broadcasted_iota(jnp.int32, cells.shape, 0)
    keep = (row < HALF) | ((row >= 32) & (row < 32 + PC - HALF))
    return row, jnp.where(keep, cells, 0.0)


def pack_kernel(tgt_ref, tgt_mass_ref, cols_ref, cells_ref, mass_ref, sems):
    x, core = lax.axis_index("x"), lax.axis_index("core")
    here = pl.ds(pl.multiple_of(x * 128, 128), 128)
    copies = (
        pltpu.make_async_copy(tgt_ref.at[:, here], cells_ref, sems.at[0]),
        pltpu.make_async_copy(tgt_mass_ref, mass_ref, sems.at[1]),
    )
    for copy in copies:
        copy.start()
    for copy in copies:
        copy.wait()
    cells = cells_ref[...]
    top = cells[0:HALF]
    bottom = jnp.concatenate([cells[HALF:PC], mass_ref[pl.ds(x, 1)], jnp.zeros((1, 128), jnp.float32)], axis=0)
    lane = lax.broadcasted_iota(jnp.int32, (HALF, 128), 1)
    first = jnp.where(lane < PIECE, top, pltpu.roll(bottom, PIECE, 1))
    second = jnp.where(lane < PIECE, pltpu.roll(top, PIECE, 1), bottom)
    piece = jnp.where(jnp.broadcast_to(core, (HALF, 128)) == 0, first, second)
    for k in range(NZ):
        cols_ref[k * HALF : (k + 1) * HALF] = piece


def stack_kernel(rows_ref, mass_ref, x_ref, own_mass_ref):
    z = lax.axis_index("z")
    for k in range(2):
        own_mass_ref[:, k * 128 : (k + 1) * 128] = mass_ref[pl.ds(2 * z + k, 1)]
    for g in range(NG):
        here = slice(g * OWN, (g + 1) * OWN)
        cells = rows_ref[g]
        norm = -0.5 * jnp.sum(cells * cells, axis=0, keepdims=True)
        ones = jnp.ones((3, OWN), jnp.float32)
        high, mid, low = pieces(cells)
        gap = jnp.zeros((8, OWN), jnp.float32)
        plus = jnp.concatenate([high[0:HALF], *pieces(norm), ones, high[HALF:PC], gap], axis=0)
        row = lax.broadcasted_iota(jnp.int32, (64, OWN), 0)
        high = jnp.where((row < HALF) | (row >= 32), plus, 0.0).astype(jnp.bfloat16)
        mid, low = (
            jnp.concatenate([part[0:HALF], gap[0:6], part[HALF:PC], gap], axis=0).astype(jnp.bfloat16)
            for part in (mid, low)
        )
        for k, part in enumerate((plus.astype(jnp.bfloat16), high, mid, mid, high, low)):
            x_ref[64 * k : 64 * (k + 1), here] = part


def gibbs_kernel(x_ref, cols_ref, mass_ref, gibbs_ref, part_ref, col_mass_ref, y_ref):
    for k in range(NG):
        part_ref[k, :, ROWS : ROWS + OWN] = mass_ref[...]
    lane = lax.broadcasted_iota(jnp.int32, (32, 128), 1)
    gap = jnp.zeros((32 - HALF, 128), jnp.float32)
    for t in range(NZ // 2):
        here = slice(t * 128, (t + 1) * 128)
        a, b = (
            jnp.concatenate([cols_ref[k * HALF : (k + 1) * HALF], gap], axis=0) for k in (2 * t, 2 * t + 1)
        )
        top = jnp.where(lane < PIECE, a, pltpu.roll(b, PIECE, 1))
        bottom = jnp.where(lane < PIECE, pltpu.roll(a, PIECE, 1), b)
        col_mass_ref[:, here] = bottom[MASS - 32 : MASS - 31]
        row, cells = masked(jnp.concatenate([top, bottom], axis=0))
        first, second, third = pieces(-0.5 * jnp.sum(cells * cells, axis=0, keepdims=True))
        high, mid, low = pieces(cells)
        extra = jnp.where(row == 29, first, jnp.where(row == 30, second, jnp.where(row == 31, third, 0.0)))
        extra = jnp.where((row >= 26) & (row < 29), 1.0, extra)
        turned = jnp.concatenate([high + extra, mid], axis=0).T.astype(jnp.bfloat16)
        y_ref[here, 0:128] = turned
        y_ref[here, 128:256] = turned
        y_ref[here, 256:384] = jnp.concatenate([low, high], axis=0).T.astype(jnp.bfloat16)
    for n in range(ROWS // 256):
        there = slice(n * 256, (n + 1) * 256)
        total = jnp.zeros((8, 256), jnp.float32)
        for m in range(COLS // 256):
            here = slice(m * 256, (m + 1) * 256)
            tile = jnp.exp(jnp.dot(y_ref[here, :], x_ref[:, there], preferred_element_type=jnp.float32))
            gibbs_ref[here, there] = tile
            total = total + jnp.sum(tile.reshape(32, 8, 256), axis=0)
        total = jnp.sum(total, axis=0, keepdims=True)
        for k in range(NG):
            part_ref[k, :, there] = total


def summed(parts_ref):
    total = parts_ref[0]
    for k in range(1, parts_ref.shape[0]):
        total = total + parts_ref[k]
    return total


def columns(gibbs_ref, scale_ref, j):
    here = slice(j * 128, (j + 1) * 128)
    total = jnp.zeros((128, 128), jnp.float32)
    for i in range(ROWS // 128):
        there = slice(i * 128, (i + 1) * 128)
        total = total + gibbs_ref[here, there] * scale_ref[:, there]
    return jnp.sum(total.T, axis=0, keepdims=True)


def column_kernel(gibbs_ref, parts_ref, part_ref, mass_ref, scale_ref):
    for k in range(NG):
        mass_ref[:, k * OWN : (k + 1) * OWN] = parts_ref[k, :, ROWS : ROWS + OWN]
    total = parts_ref[0, :, 0:ROWS]
    for k in range(1, NG):
        total = total + parts_ref[k, :, 0:ROWS]
    scale_ref[...] = mass_ref[...] / total
    for j in range(COLS // 128):
        total = columns(gibbs_ref, scale_ref, j)
        for k in range(NY):
            part_ref[k, :, j * 128 : (j + 1) * 128] = total


def relay_kernel(parts_ref, part_ref):
    total = summed(parts_ref)
    for k in range(part_ref.shape[0]):
        part_ref[k] = total


def last_column_kernel(gibbs_ref, parts_ref, mass_ref, leaving_ref, scale_ref):
    scale_ref[...] = mass_ref[...] / summed(parts_ref)
    me = lax.axis_index("x") * NC + lax.axis_index("core")
    own = scale_ref[:, pl.ds(pl.multiple_of(me * OWN, OWN), OWN)]
    for j in range(COLS // 128):
        total = columns(gibbs_ref, scale_ref, j)
        for k in (DOWN[ORDER[2 * j]], DOWN[ORDER[2 * j + 1]]):
            leaving_ref[k, :, 0:OWN] = own
            leaving_ref[k, :, OWN : OWN + 128] = total
            total = pltpu.roll(total, PIECE, 1)


def row_kernel(gibbs_ref, parts_ref, mass_ref, part_ref):
    scale = mass_ref[...] / summed(parts_ref)
    totals = [jnp.zeros((8, 128), jnp.float32)] * (ROWS // 128)
    for j in range(COLS // 128):
        here = slice(j * 128, (j + 1) * 128)
        spread = jnp.broadcast_to(scale[:, here], (128, 128)).T
        for i in range(ROWS // 128):
            there = slice(i * 128, (i + 1) * 128)
            totals[i] = totals[i] + jnp.sum((gibbs_ref[here, there] * spread).reshape(16, 8, 128), axis=0)
    for i in range(ROWS // 128):
        total = jnp.sum(totals[i], axis=0, keepdims=True)
        for k in range(NG):
            part_ref[k, :, i * 128 : (i + 1) * 128] = total


def landing_kernel(landed_ref, part_ref):
    total = landed_ref[0, :, OWN : OWN + 128]
    for k in range(1, NZ):
        total = total + landed_ref[k, :, OWN : OWN + 128]
    for k in range(NY * NG):
        part_ref[k] = total


def potential_kernel(landed_ref, parts_ref, mass_ref, rows_ref, out_ref):
    for k in range(NZ):
        rows_ref[DOWN[k]] = EPS * jnp.log(landed_ref[k, :, 0:OWN])
    lane = lax.broadcasted_iota(jnp.int32, (1, 128), 1)
    for t in range(NG // 2):
        a, b = (sum(parts_ref[y * NG + g] for y in range(NY)) for g in (2 * t, 2 * t + 1))
        total = jnp.where(lane < PIECE, a, pltpu.roll(b, PIECE, 1))
        out_ref[t : t + 1] = EPS * jnp.log(mass_ref[t : t + 1] / total)


def f32(*shape):
    return jax.ShapeDtypeStruct(shape, jnp.float32)


def call(kernel, outs, *args, scratch=(), space=pltpu.VMEM, limit=24 << 20):
    whole = pl.BlockSpec(memory_space=pltpu.VMEM)
    return pl.pallas_call(
        kernel,
        out_shape=outs,
        in_specs=[pl.BlockSpec(memory_space=space)] * len(args),
        out_specs=[whole] * len(outs),
        scratch_shapes=list(scratch),
        compiler_params=pltpu.CompilerParams(vmem_limit_bytes=limit),
    )(*args)


def swap(value, axes, groups=None):
    return lax.all_to_all(value, axes, 0, 0, tiled=True, axis_index_groups=groups)


def local(src_cells, tgt_cells, src_mass, tgt_mass):
    tgt_mass = tgt_mass.reshape(NX, 128)
    (cols,) = call(
        pack_kernel,
        (f32(NZ * HALF, 128),),
        tgt_cells,
        tgt_mass,
        scratch=[pltpu.VMEM((PC, 128), jnp.float32), pltpu.VMEM((NX, 128), jnp.float32), pltpu.SemaphoreType.DMA((2,))],
        space=pltpu.HBM,
        limit=60 << 20,
    )
    cols = swap(cols.reshape(NZ, 1, HALF * 128), "z", [ORDER]).reshape(NZ * HALF, 128)
    stack, own_mass = call(
        stack_kernel,
        (jax.ShapeDtypeStruct((384, ROWS), jnp.bfloat16), f32(1, OWN)),
        lax.all_gather(src_cells, GROUP),
        src_mass.reshape(NZ * 2, 128),
    )
    gibbs, row_parts, col_mass = call(
        gibbs_kernel,
        (f32(COLS, ROWS), f32(NG, 1, ROWS + OWN), f32(1, COLS)),
        stack,
        cols,
        own_mass,
        scratch=(pltpu.VMEM((COLS, 384), jnp.bfloat16),),
    )
    scale = pltpu.VMEM((1, ROWS), jnp.float32)
    col_parts, row_mass = call(
        column_kernel, (f32(NY, 1, COLS), f32(1, ROWS)), gibbs, swap(row_parts, GROUP), scratch=(scale,)
    )
    (col_parts,) = call(relay_kernel, (f32(NZ, 1, COLS),), swap(col_parts, "y"))
    col_parts = swap(col_parts, "z")
    (row_parts,) = call(row_kernel, (f32(NG, 1, ROWS),), gibbs, col_parts, col_mass)
    (leaving,) = call(
        last_column_kernel, (f32(NZ, 1, OWN + 128),), gibbs, swap(row_parts, GROUP), row_mass, scratch=(scale,)
    )
    landed = swap(leaving, "z", [DOWN])
    (col_parts,) = call(landing_kernel, (f32(NY * NG, 1, 128),), landed)
    row_out, col_out = call(
        potential_kernel, (f32(NZ, 1, OWN), f32(NX, 128)), landed, swap(col_parts, PLANE), tgt_mass
    )
    return row_out.reshape(NZ * OWN), col_out.reshape(NX * 128)


def solution(mesh):
    grid = Mesh(mesh.devices.reshape(NY, NX, NC, NZ), ("y", "x", "core", "z"))
    placed = (P(None, PLANE + ("z",)), P(None, "z"), P(PLANE), P("z"))
    return jax.shard_map(local, mesh=grid, in_specs=placed, out_specs=(P(PLANE), P("z")), check_vma=False)
```
